32 devices in a mesh: section: 4 (over x, core), dp: 8 (over z, y).
Axes of the slice: x: 2, y: 2, z: 4, core: 2. Of those that a mesh axis runs over, the one named last changes fastest.
Arguments:
- images: bfloat16 [2, 8, 12, 3840], P(None, 'dp'), may hold values from -6 to 6
- targets: bfloat16 [2, 8, 12, 3840], P(None, 'dp'), may hold values from -6 to 6
- kernels: bfloat16 [4, 2880, 640], P('section'), may hold values from -0.109375 to 0.109375
Outputs:
- kernel_grad: float32 [4, 2880, 640], P('section', 'dp')
The draws below stay inside these ranges and needn't reach their ends.
All inputs are finite; a program needn't handle non-finite values.
Results may differ from the reference program's by a relative error of at most 0.0075.
Values may be sent and summed in bfloat16 or wider, within the bound.
No kernel may reach another device: no remote copies, remote signals or barrier semaphores. Data moves between devices by JAX's collectives and lax.ppermute only.
A program may use at most 128 MiB of HBM per device.

```python
import jax
import jax.numpy as jnp
from jax import lax

CH = 320
CW = 640
IMG = 12
MB = 2
CEN = 6
SAMPLES = 8
KR = 2880
N_SECTION = 4


def level_of(rng, shape, split, low, largest):
    loudness, own = 1.0, jax.random.fold_in(rng, 6)
    for axis_at, blocks in split:
        draws = jnp.exp(jax.random.uniform(jax.random.fold_in(own, axis_at), (blocks,), jnp.float32, low / len(split), largest / len(split)))
        loudness = loudness * jnp.repeat(draws, shape[axis_at] // blocks).reshape([-1 if axis == axis_at else 1 for axis in range(len(shape))])
    return loudness


def normal_values(own_key, shape, deviation, bound, cuts=(), dtype=jnp.bfloat16):
    entries = deviation * jax.random.normal(own_key, shape, jnp.float32)
    if cuts:
        entries = entries * level_of(own_key, shape, cuts, -0.22, 0.18)
    return jnp.clip(entries, -bound, bound).astype(dtype)


def setup_inputs(seed: int = 0) -> dict:
    keys = jax.random.split(jax.random.key(seed), 4)
    images = normal_values(keys[0], (MB, SAMPLES, IMG, IMG * CH), 1.0, 6.0, ((1, 8),))
    targets = normal_values(keys[1], (MB, SAMPLES, IMG, IMG * CH), 1.0, 6.0, ((1, 8),))
    kernels = normal_values(keys[2], (N_SECTION, KR, CW), (9 * CH) ** -0.5, 0.109375, ((0, 4),))
    return dict(images=images, targets=targets, kernels=kernels)


def patches(tensor, stride):
    height, breadth, channels = tensor.shape
    rows_out = height // stride
    cols_out = breadth // stride
    padded = jnp.pad(tensor, ((1, 1), (1, 1), (0, 0)))
    pieces = []
    for row_tap in range(3):
        for col_tap in range(3):
            limits = (row_tap + stride * (rows_out - 1) + 1, col_tap + stride * (cols_out - 1) + 1, channels)
            pieces.append(lax.slice(padded, (row_tap, col_tap, 0), limits, (stride, stride, 1)))
    return jnp.concatenate(pieces, axis=-1).reshape(rows_out * cols_out, 9 * channels)

def unpatch(columns, height, breadth, channels):
    start_field = jnp.zeros((height, breadth, channels), jnp.float32)
    unused, pullback = jax.vjp(lambda tensor: patches(tensor, 1), start_field)
    return pullback(columns)[0]

def silu_slope(values):
    logistic = jax.nn.sigmoid(values)
    return logistic * (1.0 + values * (1.0 - logistic))

def batch_patches(grids, stride):
    return jax.vmap(lambda tensor: patches(tensor, stride))(grids)

def batch_unpatch(columns, extent, channels):
    return jax.vmap(lambda column_block: unpatch(column_block, extent, extent, channels))(columns)

def group_product(first_half, second_half, kernel):
    return jnp.concatenate([jnp.dot(first_half, kernel[:, :CH], preferred_element_type=jnp.float32), jnp.dot(second_half, kernel[:, CH:], preferred_element_type=jnp.float32)], axis=1)

def group_grad(first_half, second_half, delta):
    return jnp.concatenate([jnp.dot(first_half.T, delta[:, :CH], preferred_element_type=jnp.float32), jnp.dot(second_half.T, delta[:, CH:], preferred_element_type=jnp.float32)], axis=1)

def group_back(delta, kernel, extent):
    cells = extent * extent
    back_first = batch_unpatch(jnp.dot(delta[:, :CH], kernel[:, :CH].T, preferred_element_type=jnp.float32).reshape(SAMPLES, cells, 9 * CH), extent, CH)
    back_second = batch_unpatch(jnp.dot(delta[:, CH:], kernel[:, CH:].T, preferred_element_type=jnp.float32).reshape(SAMPLES, cells, 9 * CH), extent, CH)
    return jnp.concatenate([back_first, back_second], axis=-1)

def reference(images, targets, kernels):
    centre_cells = CEN * CEN
    full_cells = IMG * IMG
    scale_loss = 1.0 / (MB * SAMPLES)
    grads_list = [jnp.zeros((9 * CH, CW), jnp.float32) for section_number in range(4)]
    for micro_batch in range(MB):
        image_grid = images[micro_batch].reshape(SAMPLES, IMG, IMG, CH)
        target_rows = targets[micro_batch].reshape(SAMPLES * full_cells, CH).astype(jnp.float32)
        encoder_cols = batch_patches(image_grid, 2).reshape(SAMPLES * centre_cells, 9 * CH)
        encoder_pre = jnp.dot(encoder_cols, kernels[0], preferred_element_type=jnp.float32)
        encoded = jax.nn.silu(encoder_pre).astype(jnp.bfloat16)
        hidden = encoded
        saved = []
        for centre_level in (1, 2):
            lattice = hidden.reshape(SAMPLES, CEN, CEN, CW)
            first_half = batch_patches(lattice[..., :CH], 1).reshape(SAMPLES * centre_cells, 9 * CH)
            second_half = batch_patches(lattice[..., CH:], 1).reshape(SAMPLES * centre_cells, 9 * CH)
            preact = group_product(first_half, second_half, kernels[centre_level])
            saved.append((first_half, second_half, preact))
            hidden = (hidden.astype(jnp.float32) + jax.nn.silu(preact)).astype(jnp.bfloat16)
        joined = (hidden.astype(jnp.float32) + encoded.astype(jnp.float32)).astype(jnp.bfloat16)
        upsampled = jnp.repeat(jnp.repeat(joined.reshape(SAMPLES, CEN, CEN, CW), 2, axis=1), 2, axis=2)
        dec_first = batch_patches(upsampled[..., :CH], 1).reshape(SAMPLES * full_cells, 9 * CH)
        dec_second = batch_patches(upsampled[..., CH:], 1).reshape(SAMPLES * full_cells, 9 * CH)
        decoder_pre = group_product(dec_first, dec_second, kernels[3])
        value_dec = decoder_pre[:, :CH]
        gate_dec = decoder_pre[:, CH:]
        residual = (value_dec * jax.nn.silu(gate_dec) - target_rows) * scale_loss
        delta_dec = jnp.concatenate([residual * jax.nn.silu(gate_dec), residual * value_dec * silu_slope(gate_dec)], axis=1).astype(jnp.bfloat16)
        grads_list[3] = grads_list[3] + group_grad(dec_first, dec_second, delta_dec)
        back_up = group_back(delta_dec, kernels[3], IMG)
        joined_grad = back_up.reshape(SAMPLES, CEN, 2, CEN, 2, CW).sum(axis=(2, 4)).reshape(SAMPLES * centre_cells, CW).astype(jnp.bfloat16)
        grad_hidden = joined_grad
        for centre_level in (2, 1):
            first_half, second_half, preact = saved[centre_level - 1]
            delta_centre = (grad_hidden.astype(jnp.float32) * silu_slope(preact)).astype(jnp.bfloat16)
            grads_list[centre_level] = grads_list[centre_level] + group_grad(first_half, second_half, delta_centre)
            back_all = group_back(delta_centre, kernels[centre_level], CEN).reshape(SAMPLES * centre_cells, CW)
            grad_hidden = (grad_hidden.astype(jnp.float32) + back_all).astype(jnp.bfloat16)
        grad_encoded = grad_hidden.astype(jnp.float32) + joined_grad.astype(jnp.float32)
        delta_enc = (grad_encoded * silu_slope(encoder_pre)).astype(jnp.bfloat16)
        grads_list[0] = grads_list[0] + group_grad(encoder_cols, encoder_cols, delta_enc)
    return jnp.stack(grads_list)
```

```python
import functools

import jax
import jax.numpy as jnp
import numpy as np
from jax import lax
from jax.experimental import pallas as pl
from jax.experimental.pallas import tpu as pltpu
from jax.sharding import PartitionSpec as P

BF = jnp.bfloat16
F32 = jnp.float32
TAPS = [(a, b) for a in range(3) for b in range(3)]
PARITIES = [(r, s) for r in range(2) for s in range(2)]


def offset_of(parity, tap):
    return (parity + tap - 1) // 2


def dot(left, right, dims=((1,), (0,))):
    return lax.dot_general(left, right, (dims, ((), ())), preferred_element_type=F32)


def dot_nt(left, right):
    return dot(left, right, ((1,), (1,)))


def dot_tn(left, right):
    return dot(left, right, ((0,), (0,)))


def sigmoid(v):
    return 1.0 / (1.0 + jnp.exp(-v))


def silu(v):
    return v * sigmoid(v)


def slope(v):
    g = sigmoid(v)
    return g * (1.0 + v * (1.0 - g))


class Sizes:
    def __init__(self, images, kernel, dp):
        self.micro = images.shape[0]
        self.full = images.shape[2]
        self.half = self.full // 2
        self.taps_rows, self.width = kernel.shape
        self.chan = self.taps_rows // 9
        self.cells = self.half * self.half
        self.used = self.micro * self.cells
        self.rows = -(-self.used // 16) * 16
        self.group = self.width // 2
        self.low = -(-self.group // 128) * 128
        self.high = self.group // 128 * 128
        self.fine = self.micro * self.full * self.full
        self.dp = dp
        self.share = self.taps_rows // dp


def selectors(z):
    rows, n = z.rows, z.half

    def at(m, i, j):
        return m * z.cells + i * n + j

    shift = np.zeros((9, rows, rows), np.float32)
    enc = np.zeros((9, rows, z.fine), np.float32)
    parity = np.zeros((4, rows, z.fine), np.float32)
    gather = np.zeros((9, rows, 4, rows), np.float32)
    for m in range(z.micro):
        for i in range(n):
            for j in range(n):
                r = at(m, i, j)
                for t, (a, b) in enumerate(TAPS):
                    ii, jj = i + a - 1, j + b - 1
                    if 0 <= ii < n and 0 <= jj < n:
                        shift[t, r, at(m, ii, jj)] = 1
                    ii, jj = 2 * i + a - 1, 2 * j + b - 1
                    if 0 <= ii < z.full and 0 <= jj < z.full:
                        enc[t, r, (m * z.full + ii) * z.full + jj] = 1
                    for p, (pr, ps) in enumerate(PARITIES):
                        ii, jj = i + offset_of(pr, a), j + offset_of(ps, b)
                        if 0 <= ii < n and 0 <= jj < n:
                            gather[t, at(m, ii, jj), p, r] = 1
                for p, (pr, ps) in enumerate(PARITIES):
                    parity[p, r, (m * z.full + 2 * i + pr) * z.full + 2 * j + ps] = 1
    back = shift.transpose(0, 2, 1)
    return dict(
        shift=shift.reshape(9 * rows, rows),
        back=back.reshape(9 * rows, rows),
        enc=enc.reshape(9 * rows, z.fine),
        parity=parity.reshape(4 * rows, z.fine),
        gather=gather.reshape(9 * rows, 4 * rows),
    )


def lanes(shape):
    return lax.broadcasted_iota(jnp.int32, shape, 1)


def join_columns(z, first, second):
    overlap = z.low - z.high
    if overlap == 0:
        return jnp.concatenate([first, second], axis=1)
    mid_first = first[:, z.high :]
    mid = jnp.where(lanes(mid_first.shape) < z.group - z.high, mid_first, second[:, :overlap])
    return jnp.concatenate([first[:, : z.high], mid, second[:, overlap:]], axis=1)


def split_groups(z, value):
    swapped = pltpu.roll(value.astype(F32), z.group, 1).astype(BF)
    return value[:, : z.group], swapped[:, : z.group]


def tap_rows(z, t):
    return slice(t * z.rows, (t + 1) * z.rows)


def tap_kernel(z, kernel, t, low):
    rows = pl.ds(t * z.chan, z.chan)
    return kernel[rows, : z.low] if low else kernel[rows, z.high :]


def conv_forward(z, value, kernel, shift):
    first, second = split_groups(z, value)
    first = dot(shift[...], first).astype(BF)
    second = dot(shift[...], second).astype(BF)
    total_first = total_second = None
    for t in range(9):
        a = dot(first[tap_rows(z, t)], tap_kernel(z, kernel, t, True))
        b = dot(second[tap_rows(z, t)], tap_kernel(z, kernel, t, False))
        total_first = a if total_first is None else total_first + a
        total_second = b if total_second is None else total_second + b
    return join_columns(z, total_first, total_second)


def join_groups(z, first, second, scratch):
    scratch[0, :, : z.group] = first
    scratch[1, :, : z.group] = second
    left = scratch[0]
    right = pltpu.roll(scratch[1], z.group, 1)
    return jnp.where(lanes(left.shape) < z.group, left, right)


def rows_times_kernel(z, first, second, kernel, scratch):
    total_first = total_second = None
    for t in range(9):
        a = dot_nt(first[tap_rows(z, t)], tap_kernel(z, kernel, t, True))
        b = dot_nt(second[tap_rows(z, t)], tap_kernel(z, kernel, t, False))
        total_first = a if total_first is None else total_first + a
        total_second = b if total_second is None else total_second + b
    return join_groups(z, total_first, total_second, scratch)


def conv_backward(z, delta, kernel, back, scratch):
    first = delta[:, : z.low].astype(F32)
    first = jnp.where(lanes(first.shape) < z.group, first, 0.0).astype(BF)
    second = delta[:, z.high :].astype(F32)
    second = jnp.where(lanes(second.shape) >= z.group - z.high, second, 0.0).astype(BF)
    first = dot(back[...], first).astype(BF)
    second = dot(back[...], second).astype(BF)
    return rows_times_kernel(z, first, second, kernel, scratch)


def encoder_kernel(z, images, kernel, enc, out, patches_out):
    columns = dot(enc[...], images[...]).astype(BF)
    total = None
    for t in range(9):
        part = columns[tap_rows(z, t)]
        patches_out[t, :, : z.chan] = part
        a = dot(part, kernel[pl.ds(t * z.chan, z.chan), :])
        total = a if total is None else total + a
    out[0] = silu(total).astype(BF)
    out[1] = slope(total).astype(BF)


def centre_kernel(z, inbound, kernel, shift, out, slope_out):
    value = inbound[0]
    preact = conv_forward(z, value, kernel, shift)
    out[0] = value
    out[1] = (value.astype(F32) + silu(preact)).astype(BF)
    slope_out[...] = slope(preact)


def middle_kernel(
    z, scale, inbound, centre, decoder, targets, shift, back, parity, gather,
    grads, kept, sums, joined_out, scratch, delta_p, delta_q, sums_p, sums_q,
):
    scratch[...] = jnp.zeros_like(scratch)
    encoded = inbound[0]
    hidden = inbound[1]
    preact = conv_forward(z, hidden, centre, shift)
    hidden3 = (hidden.astype(F32) + silu(preact)).astype(BF)
    joined = (hidden3.astype(F32) + encoded.astype(F32)).astype(BF)
    joined_out[...] = joined
    first, second = split_groups(z, joined)
    first = dot(shift[...], first).astype(BF)
    second = dot(shift[...], second).astype(BF)
    total_p = [None] * 4
    total_q = [None] * 4
    for t, (a, b) in enumerate(TAPS):
        shifts = sorted({(offset_of(r, a), offset_of(s, b)) for r, s in PARITIES})
        blocks = [tap_rows(z, (i + 1) * 3 + j + 1) for i, j in shifts]
        left_p = jnp.concatenate([first[block] for block in blocks], axis=0)
        left_q = jnp.concatenate([second[block] for block in blocks], axis=0)
        part_p = dot(left_p, tap_kernel(z, decoder, t, True))
        part_q = dot(left_q, tap_kernel(z, decoder, t, False))
        for p, (r, s) in enumerate(PARITIES):
            at = tap_rows(z, shifts.index((offset_of(r, a), offset_of(s, b))))
            total_p[p] = part_p[at] if total_p[p] is None else total_p[p] + part_p[at]
            total_q[p] = part_q[at] if total_q[p] is None else total_q[p] + part_q[at]
    wanted = dot(parity[...], targets[...])
    move = z.group - z.high
    delta_p[...] = jnp.zeros_like(delta_p)
    delta_q[...] = jnp.zeros_like(delta_q)
    for p in range(4):
        value = total_p[p][:, : z.group]
        gate = total_q[p]
        if move:
            gate = pltpu.roll(gate, z.low - move, 1)
        gate = gate[:, : z.group]
        act = silu(gate)
        residual = (value * act - wanted[tap_rows(z, p)]) * scale
        delta_p[tap_rows(z, p), : z.group] = residual * act
        delta_q[tap_rows(z, p), : z.group] = residual * value * slope(gate)
    moved = delta_q[...]
    if move:
        moved = pltpu.roll(moved, move, 1)
    sums_p[...] = dot(gather[...], delta_p[...].astype(BF)).astype(BF)
    sums_q[...] = dot(gather[...], moved.astype(BF)).astype(BF)
    for t in range(9):
        part_p = sums_p[tap_rows(z, t)].astype(F32)
        part_q = sums_q[tap_rows(z, t)].astype(F32)
        sums[t] = join_columns(z, part_p, part_q).astype(BF)
    grad = rows_times_kernel(z, sums_p, sums_q, decoder, scratch).astype(BF)
    delta = (grad.astype(F32) * slope(preact)).astype(BF)
    flow = conv_backward(z, delta, centre, back, scratch)
    grads[0] = (grad.astype(F32) + flow).astype(BF)
    grads[1] = grad
    kept[0] = delta
    kept[1] = hidden


def centre_back_kernel(z, grads, enc_slope, centre_slope, kernel, back, out, delta_out, scratch):
    scratch[...] = jnp.zeros_like(scratch)
    above = grads[0].astype(F32)
    delta = (above * centre_slope[...]).astype(BF)
    delta_out[...] = delta
    flow = conv_backward(z, delta, kernel, back, scratch)
    below = (above + flow).astype(BF)
    total = below.astype(F32) + grads[1].astype(F32)
    out[...] = (total * enc_slope[1].astype(F32)).astype(BF)


def partner_of(z, place, k, relative):
    if not relative:
        return k
    return place ^ k


def first_tap(z, dest):
    return dest * z.share // z.chan


def prepare_kernel(z, relative, where, patches, encoded, kept_in, joined, deep, delta, sums, *outs):
    section, place = where[0], where[1]
    n = z.dp
    left, right, extra = outs[:n], outs[n : 2 * n], outs[2 * n :]

    @pl.when(section == 0)
    def _():
        for k in range(n):
            tap = first_tap(z, partner_of(z, place, k, relative))
            near = patches[tap].astype(F32)
            far = patches[jnp.minimum(tap + 1, 8)].astype(F32)
            both = jnp.where(lanes(near.shape) < z.chan, near, pltpu.roll(far, z.chan, 1))
            left[k][...] = both.astype(BF)
            right[k][...] = deep[...]

    @pl.when(section == 1)
    def _():
        for k in range(n):
            left[k][...] = encoded[0]
            right[k][...] = delta[...]

    @pl.when(section == 2)
    def _():
        for k in range(n):
            left[k][...] = kept_in[1]
            right[k][...] = kept_in[0]

    @pl.when(section == 3)
    def _():
        for k in range(n):
            tap = first_tap(z, partner_of(z, place, k, relative))
            left[k][...] = joined[...]
            right[k][...] = sums[tap]
            extra[k][...] = sums[jnp.minimum(tap + 1, 8)]


def weight_kernel(z, where, shift, *refs):
    n = z.dp
    left, right, extra = refs[:n], refs[n : 2 * n], refs[2 * n : 3 * n]
    out, lefts, rights, rows_out = refs[3 * n :]
    section, place = where[0], where[1]
    tap = first_tap(z, place)

    def stack(target, pieces):
        for k in range(n):
            target[pl.ds(k * z.rows, z.rows), :] = pieces[k][...]

    def grouped(at):
        overlap = z.low - z.high
        first = dot_tn(lefts[:, : z.low], rights[:, : z.low])
        second = dot_tn(lefts[:, z.high :], rights[:, z.high :])
        move = z.group - z.high
        both = join_columns(z, first[: z.chan], second[move : move + z.chan])
        rows_out[pl.ds(at * z.chan, z.chan), :] = both

    @pl.when(section == 0)
    def _():
        stack(lefts, left)
        stack(rights, right)
        rows_out[...] = dot_tn(lefts[...], rights[...])

    @pl.when(jnp.logical_or(section == 1, section == 2))
    def _():
        stack(rights, right)
        for at in range(2):
            here = jnp.minimum(tap + at, 8)
            move = shift[pl.ds(pl.multiple_of(here * z.rows, 16), z.rows), :]
            for k in range(n):
                lefts[pl.ds(k * z.rows, z.rows), :] = dot(move, left[k][...]).astype(BF)
            grouped(at)

    @pl.when(section == 3)
    def _():
        stack(lefts, left)
        stack(rights, right)
        grouped(0)
        stack(rights, extra)
        grouped(1)

    begin = place * z.share - tap * z.chan
    if z.share % 8 == 0 and z.chan % 8 == 0:
        out[...] = rows_out[pl.ds(pl.multiple_of(begin, 8), z.share), :]
    else:
        size = -(-(z.share + 7) // 8) * 8
        rest = lax.rem(begin, 8)
        block = rows_out[pl.ds(pl.multiple_of(begin - rest, 8), size), :]
        out[...] = pltpu.roll(block, lax.rem(size - rest, size), 0)[: z.share]


def call(body, outs, scratch=(), smem=False, n_in=1, flops=10**9):
    specs = [pl.BlockSpec(memory_space=pltpu.VMEM)] * n_in
    if smem:
        specs[0] = pl.BlockSpec(memory_space=pltpu.SMEM)
    single = not isinstance(outs, (list, tuple))
    return pl.pallas_call(
        body,
        out_shape=outs,
        in_specs=specs,
        out_specs=pl.BlockSpec(memory_space=pltpu.VMEM)
        if single
        else [pl.BlockSpec(memory_space=pltpu.VMEM)] * len(outs),
        scratch_shapes=list(scratch),
        compiler_params=pltpu.CompilerParams(vmem_limit_bytes=40 * 2**20),
    )


def exchange(z, relative, pieces):
    n = z.dp
    if not relative:
        stacked = lax.all_to_all(jnp.stack(pieces), "dp", 0, 0, tiled=True)
        return [stacked[k] for k in range(n)]
    return [pieces[0]] + [
        lax.ppermute(pieces[k], "dp", [(d, d ^ k) for d in range(n)]) for k in range(1, n)
    ]


def on_device(images, targets, kernels):
    kernel = kernels[0]
    dp = lax.axis_size("dp")
    n_section = lax.axis_size("section")
    z = Sizes(images, kernel, dp)
    relative = dp <= 16 and dp & (dp - 1) == 0
    sel = {k: jnp.asarray(v, BF) for k, v in selectors(z).items()}
    scale = 1.0 / (z.micro * dp * images.shape[1])
    where = jnp.stack([lax.axis_index("section"), lax.axis_index("dp")]).astype(jnp.int32)
    image_rows = images.reshape(z.fine, z.chan)
    target_rows = targets.reshape(z.fine, z.chan)
    rows, width = z.rows, z.width
    pair = jax.ShapeDtypeStruct((2, rows, width), BF)
    one = jax.ShapeDtypeStruct((rows, width), BF)
    nine = jax.ShapeDtypeStruct((9, rows, width), BF)
    join = pltpu.VMEM((2, rows, width), F32)

    def across(x, bit):
        return lax.ppermute(x, "section", [(s, s ^ bit) for s in range(n_section)])

    other = across(kernel, 1)
    encoded, patches = call(functools.partial(encoder_kernel, z), [pair, nine], n_in=3)(
        image_rows, kernel, sel["enc"]
    )
    encoded_in = across(encoded, 1)
    forward, centre_slope = call(
        functools.partial(centre_kernel, z),
        [pair, jax.ShapeDtypeStruct((rows, width), F32)],
        n_in=3,
    )(encoded_in, kernel, sel["shift"])
    forward_in = across(forward, 2)
    grads, kept, sums, joined = call(
        functools.partial(middle_kernel, z, scale),
        [pair, pair, nine, one],
        scratch=[
            join,
            pltpu.VMEM((4 * rows, z.low), F32),
            pltpu.VMEM((4 * rows, z.low), F32),
            pltpu.VMEM((9 * rows, z.low), BF),
            pltpu.VMEM((9 * rows, z.width - z.high), BF),
        ],
        n_in=8,
    )(forward_in, other, kernel, target_rows, sel["shift"], sel["back"], sel["parity"], sel["gather"])
    grads_in = across(grads, 2)
    kept_in = across(kept, 1)
    deep, delta = call(functools.partial(centre_back_kernel, z), [one, one], scratch=[join], n_in=5)(
        grads_in, encoded_in, centre_slope, kernel, sel["back"]
    )
    deep_in = across(deep, 1)
    pieces = call(
        functools.partial(prepare_kernel, z, relative), [one] * (3 * dp), smem=True, n_in=8
    )(where, patches, encoded_in, kept_in, joined, deep_in, delta, sums)
    left = exchange(z, relative, pieces[:dp])
    right = exchange(z, relative, pieces[dp : 2 * dp])
    extra = exchange(z, relative, pieces[2 * dp :])
    out = call(
        functools.partial(weight_kernel, z),
        jax.ShapeDtypeStruct((z.share, width), F32),
        scratch=[
            pltpu.VMEM((dp * rows, width), BF),
            pltpu.VMEM((dp * rows, width), BF),
            pltpu.VMEM((2 * z.chan, width), F32),
        ],
        smem=True,
        n_in=2 + 3 * dp,
    )(where, sel["shift"], *left, *right, *extra)
    return out[None]


def solution(mesh):
    return jax.shard_map(
        on_device,
        mesh=mesh,
        in_specs=(P(None, "dp", None, None), P(None, "dp", None, None), P("section", None, None)),
        out_specs=P("section", "dp", None),
        check_vma=False,
    )
```

```python
import functools

import jax
import jax.numpy as jnp
import numpy as np
from jax import lax
from jax.experimental import pallas as pl
from jax.experimental.pallas import tpu as pltpu
from jax.sharding import PartitionSpec as P

BF = jnp.bfloat16
F32 = jnp.float32
TAPS = [(a, b) for a in range(3) for b in range(3)]
PARITIES = [(r, s) for r in range(2) for s in range(2)]


def offset_of(parity, tap):
    return (parity + tap - 1) // 2


def dot(left, right, dims=((1,), (0,))):
    return lax.dot_general(left, right, (dims, ((), ())), preferred_element_type=F32)


def dot_nt(left, right):
    return dot(left, right, ((1,), (1,)))


def dot_tn(left, right):
    return dot(left, right, ((0,), (0,)))


def sigmoid(v):
    return 1.0 / (1.0 + jnp.exp(-v))


def silu(v):
    return v * sigmoid(v)


def slope(v):
    g = sigmoid(v)
    return g * (1.0 + v * (1.0 - g))


class Sizes:
    def __init__(self, images, kernel, dp):
        self.micro = images.shape[0]
        self.full = images.shape[2]
        self.half = self.full // 2
        self.taps_rows, self.width = kernel.shape
        self.chan = self.taps_rows // 9
        self.cells = self.half * self.half
        self.rows = -(-self.cells // 8) * 8
        self.both = self.micro * self.rows
        self.group = self.width // 2
        self.low = -(-self.group // 128) * 128
        self.high = self.group // 128 * 128
        self.fine = self.full * self.full
        self.dp = dp
        self.share = self.taps_rows // dp


def selectors(z):
    rows, n = z.rows, z.half
    shift = np.zeros((9, rows, rows), np.float32)
    enc = np.zeros((9, z.micro, rows, z.micro, z.fine), np.float32)
    parity = np.zeros((4, rows, z.fine), np.float32)
    gather = np.zeros((9, rows, 4, rows), np.float32)
    for i in range(n):
        for j in range(n):
            r = i * n + j
            for t, (a, b) in enumerate(TAPS):
                ii, jj = i + a - 1, j + b - 1
                if 0 <= ii < n and 0 <= jj < n:
                    shift[t, r, ii * n + jj] = 1
                ii, jj = 2 * i + a - 1, 2 * j + b - 1
                if 0 <= ii < z.full and 0 <= jj < z.full:
                    for m in range(z.micro):
                        enc[t, m, r, m, ii * z.full + jj] = 1
                for p, (pr, ps) in enumerate(PARITIES):
                    ii, jj = i + offset_of(pr, a), j + offset_of(ps, b)
                    if 0 <= ii < n and 0 <= jj < n:
                        gather[t, ii * n + jj, p, r] = 1
            for p, (pr, ps) in enumerate(PARITIES):
                parity[p, r, (2 * i + pr) * z.full + 2 * j + ps] = 1
    back = shift.transpose(0, 2, 1)
    return dict(
        shift=shift.reshape(9 * rows, rows),
        back=back.reshape(9 * rows, rows),
        enc=enc.reshape(9 * z.both, z.micro * z.fine),
        parity=parity.reshape(4 * rows, z.fine),
        gather=gather.reshape(9 * rows, 4 * rows),
    )


def lanes(shape):
    return lax.broadcasted_iota(jnp.int32, shape, 1)


def join_columns(z, first, second):
    overlap = z.low - z.high
    if overlap == 0:
        return jnp.concatenate([first, second], axis=1)
    mid_first = first[:, z.high :]
    mid = jnp.where(lanes(mid_first.shape) < z.group - z.high, mid_first, second[:, :overlap])
    return jnp.concatenate([first[:, : z.high], mid, second[:, overlap:]], axis=1)


def split_groups(z, value):
    swapped = pltpu.roll(value.astype(F32), z.group, 1).astype(BF)
    return value[:, : z.group], swapped[:, : z.group]


def tap_rows(z, t):
    return slice(t * z.rows, (t + 1) * z.rows)


class Weights:
    def __init__(self, z, mine, own, other, buffer, sems):
        self.z, self.buffer, self.seen = z, buffer, set()

        def copies(source):
            for t in range(9):
                rows = pl.ds(t * z.chan, z.chan)
                yield pltpu.make_async_copy(source.at[rows], buffer.at[rows], sems.at[t])

        self.waits = list(copies(own))
        if mine is None:
            for copy in self.waits:
                copy.start()
            return

        @pl.when(mine)
        def _():
            for copy in copies(own):
                copy.start()

        @pl.when(jnp.logical_not(mine))
        def _():
            for copy in copies(other):
                copy.start()

    def tap(self, t, columns=slice(None)):
        if t not in self.seen:
            self.seen.add(t)
            self.waits[t].wait()
        return self.buffer[pl.ds(t * self.z.chan, self.z.chan), columns]

    def first(self, t):
        return self.tap(t, slice(0, self.z.low))

    def second(self, t):
        return self.tap(t, slice(self.z.high, self.z.width))


def conv_forward(z, value, weights, shift):
    first, second = split_groups(z, value)
    first = dot(shift[...], first).astype(BF)
    second = dot(shift[...], second).astype(BF)
    total_first = total_second = None
    for t in range(9):
        a = dot(first[tap_rows(z, t)], weights.first(t))
        b = dot(second[tap_rows(z, t)], weights.second(t))
        total_first = a if total_first is None else total_first + a
        total_second = b if total_second is None else total_second + b
    return join_columns(z, total_first, total_second)


def join_groups(z, first, second, scratch):
    scratch[0, :, : z.group] = first
    scratch[1, :, : z.group] = second
    left = scratch[0]
    right = pltpu.roll(scratch[1], z.group, 1)
    return jnp.where(lanes(left.shape) < z.group, left, right)


def rows_times_kernel(z, first, second, weights, scratch):
    total_first = total_second = None
    for t in range(9):
        a = dot_nt(first[tap_rows(z, t)], weights.first(t))
        b = dot_nt(second[tap_rows(z, t)], weights.second(t))
        total_first = a if total_first is None else total_first + a
        total_second = b if total_second is None else total_second + b
    return join_groups(z, total_first, total_second, scratch)


def conv_backward(z, delta, weights, back, scratch):
    first = delta[:, : z.low].astype(F32)
    first = jnp.where(lanes(first.shape) < z.group, first, 0.0).astype(BF)
    second = delta[:, z.high :].astype(F32)
    second = jnp.where(lanes(second.shape) >= z.group - z.high, second, 0.0).astype(BF)
    first = dot(back[...], first).astype(BF)
    second = dot(back[...], second).astype(BF)
    return rows_times_kernel(z, first, second, weights, scratch)


def encoder_kernel(z, kernel, images, enc, out, patches_out, buffer, sems):
    weights = Weights(z, None, kernel, None, buffer, sems)
    columns = dot(enc[...], images[...]).astype(BF)
    total = None
    for t in range(9):
        part = columns[t * z.both : (t + 1) * z.both]
        patches_out[t, :, : z.chan] = part
        a = dot(part, weights.tap(t))
        total = a if total is None else total + a
    encoded = silu(total).astype(BF)
    steep = slope(total).astype(BF)
    for m in range(z.micro):
        out[m] = encoded[m * z.rows : (m + 1) * z.rows]
        out[z.micro + m] = steep[m * z.rows : (m + 1) * z.rows]


def centre_kernel(z, where, kernel, other, own, received, shift, out, slope_out, enc_slope_out, buffer, sems):
    odd = lax.rem(where[0], 2) == 1
    weights = Weights(z, odd, kernel, other, buffer, sems)
    value = jnp.where(odd, received[1].astype(F32), own[0].astype(F32)).astype(BF)
    enc_slope_out[...] = jnp.where(odd, received[3].astype(F32), own[2].astype(F32))
    preact = conv_forward(z, value, weights, shift)
    out[0] = value
    out[1] = (value.astype(F32) + silu(preact)).astype(BF)
    slope_out[...] = slope(preact)


def middle_kernel(
    z, scale, where, kernel, other, inbound, targets, shift, back, parity, gather,
    grads, own_out, send, scratch, delta_p, delta_q, sums_p, sums_q, buffer2, buffer3, sems2, sems3,
):
    odd = lax.rem(where[0], 2) == 1
    centre = Weights(z, jnp.logical_not(odd), kernel, other, buffer2, sems2)
    decoder = Weights(z, odd, kernel, other, buffer3, sems3)
    scratch[...] = jnp.zeros_like(scratch)
    encoded = inbound[0]
    hidden = inbound[1]
    preact = conv_forward(z, hidden, centre, shift)
    hidden3 = (hidden.astype(F32) + silu(preact)).astype(BF)
    joined = (hidden3.astype(F32) + encoded.astype(F32)).astype(BF)
    first, second = split_groups(z, joined)
    first = dot(shift[...], first).astype(BF)
    second = dot(shift[...], second).astype(BF)
    total_p = [None] * 4
    total_q = [None] * 4
    for t, (a, b) in enumerate(TAPS):
        shifts = sorted({(offset_of(r, a), offset_of(s, b)) for r, s in PARITIES})
        blocks = [tap_rows(z, (i + 1) * 3 + j + 1) for i, j in shifts]
        left_p = jnp.concatenate([first[block] for block in blocks], axis=0)
        left_q = jnp.concatenate([second[block] for block in blocks], axis=0)
        part_p = dot(left_p, decoder.first(t))
        part_q = dot(left_q, decoder.second(t))
        for p, (r, s) in enumerate(PARITIES):
            at = tap_rows(z, shifts.index((offset_of(r, a), offset_of(s, b))))
            total_p[p] = part_p[at] if total_p[p] is None else total_p[p] + part_p[at]
            total_q[p] = part_q[at] if total_q[p] is None else total_q[p] + part_q[at]
    wanted = dot(parity[...], targets[lax.rem(where[0], 2)])
    move = z.group - z.high
    delta_p[...] = jnp.zeros_like(delta_p)
    delta_q[...] = jnp.zeros_like(delta_q)
    for p in range(4):
        value = total_p[p][:, : z.group]
        gate = total_q[p]
        if move:
            gate = pltpu.roll(gate, z.low - move, 1)
        gate = gate[:, : z.group]
        act = silu(gate)
        residual = (value * act - wanted[tap_rows(z, p)]) * scale
        delta_p[tap_rows(z, p), : z.group] = residual * act
        delta_q[tap_rows(z, p), : z.group] = residual * value * slope(gate)
    moved = delta_q[...]
    if move:
        moved = pltpu.roll(moved, move, 1)
    sums_p[...] = dot(gather[...], delta_p[...].astype(BF)).astype(BF)
    sums_q[...] = dot(gather[...], moved.astype(BF)).astype(BF)
    grad = rows_times_kernel(z, sums_p, sums_q, decoder, scratch).astype(BF)
    delta = (grad.astype(F32) * slope(preact)).astype(BF)
    flow = conv_backward(z, delta, centre, back, scratch)
    grads[0] = (grad.astype(F32) + flow).astype(BF)
    grads[1] = grad

    def sums(t):
        part_p = sums_p[tap_rows(z, t)].astype(F32)
        part_q = sums_q[tap_rows(z, t)].astype(F32)
        return join_columns(z, part_p, part_q).astype(BF)

    @pl.when(odd)
    def _():
        for t in range(9):
            own_out[t] = sums(t)
        own_out[9] = joined
        send[0] = delta
        send[1] = hidden

    @pl.when(jnp.logical_not(odd))
    def _():
        for t in range(9):
            send[t] = sums(t)
        own_out[0] = delta
        own_out[1] = hidden
        own_out[9] = joined


def centre_back_kernel(
    z, where, kernel, other, grads, enc_slope, centre_slope, back, own_out, send, scratch, buffer, sems
):
    odd = lax.rem(where[0], 2) == 1
    weights = Weights(z, odd, kernel, other, buffer, sems)
    scratch[...] = jnp.zeros_like(scratch)
    above = grads[0].astype(F32)
    delta = (above * centre_slope[...]).astype(BF)
    flow = conv_backward(z, delta, weights, back, scratch)
    below = (above + flow).astype(BF)
    total = below.astype(F32) + grads[1].astype(F32)
    deep = total * enc_slope[...]
    own_out[...] = jnp.where(odd, delta.astype(F32), deep).astype(BF)
    send[...] = jnp.where(odd, deep, delta.astype(F32)).astype(BF)


def first_tap(z, dest):
    return dest * z.share // z.chan


def prepare_first_kernel(z, where, patches, own, received, middle_own, middle_received, out, joined):
    section = where[0]
    n, rows = z.dp, z.rows

    @pl.when(section == 0)
    def _():
        for k in range(n):
            tap = first_tap(z, k)
            near = patches[tap].astype(F32)
            far = patches[min(tap + 1, 8)].astype(F32)
            both = jnp.where(lanes(near.shape) < z.chan, near, pltpu.roll(far, z.chan, 1))
            out[k] = both.astype(BF)

    @pl.when(section == 1)
    def _():
        for k in range(n):
            out[k, :rows] = received[0]
            out[k, rows:] = received[1]

    @pl.when(section == 2)
    def _():
        for k in range(n):
            out[k, :rows] = middle_own[1]
            out[k, rows:] = middle_received[1]

    @pl.when(section == 3)
    def _():
        for k in range(n):
            tap = first_tap(z, k)
            out[k, :rows] = middle_received[tap]
            out[k, rows:] = middle_own[tap]

    for k in range(n):
        joined[k] = middle_own[9]


def prepare_second_kernel(z, where, back_own, back_received, middle_own, middle_received, out):
    section = where[0]
    n, rows = z.dp, z.rows

    def fill(top, bottom):
        for k in range(n):
            out[k, :rows] = top[...]
            out[k, rows:] = bottom[...]

    pl.when(section == 0)(lambda: fill(back_own, back_received))
    pl.when(section == 1)(lambda: fill(back_received, back_own))
    pl.when(section == 2)(lambda: fill(middle_own.at[0], middle_received.at[0]))

    @pl.when(section == 3)
    def _():
        for k in range(n):
            tap = min(first_tap(z, k) + 1, 8)
            out[k, :rows] = middle_received[tap]
            out[k, rows:] = middle_own[tap]


def weight_kernel(z, where, shift, left, right, joined, joined_received, out, lefts, rows_out):
    n = z.dp
    section, place = where[0], where[1]
    tap = first_tap(z, place)
    total = n * z.both

    def grouped(at, pairs):
        first = second = None
        for a, b in pairs:
            one = dot_tn(a[:, : z.low], b[:, : z.low])
            two = dot_tn(a[:, z.high :], b[:, z.high :])
            first = one if first is None else first + one
            second = two if second is None else second + two
        move = z.group - z.high
        both = join_columns(z, first[: z.chan], second[move : move + z.chan])
        rows_out[pl.ds(at * z.chan, z.chan), :] = both

    @pl.when(section == 0)
    def _():
        a = left[...].reshape(total, z.width)
        b = right[...].reshape(total, z.width)
        rows_out[...] = dot_tn(a, b)

    @pl.when(jnp.logical_or(section == 1, section == 2))
    def _():
        for at in range(2):
            here = jnp.minimum(tap + at, 8)
            move = shift[pl.ds(pl.multiple_of(here * z.rows, 8), z.rows), :]
            for k in range(n):
                for m in range(z.micro):
                    part = left[k, pl.ds(m * z.rows, z.rows)]
                    lefts[pl.ds((k * z.micro + m) * z.rows, z.rows), :] = dot(move, part).astype(BF)
            grouped(at, [(lefts[...], right[...].reshape(total, z.width))])

    @pl.when(section == 3)
    def _():
        for k in range(n):
            lefts[pl.ds(k * z.both, z.rows), :] = joined_received[k]
            lefts[pl.ds(k * z.both + z.rows, z.rows), :] = joined[k]
        grouped(0, [(lefts[...], left[...].reshape(total, z.width))])
        grouped(1, [(lefts[...], right[...].reshape(total, z.width))])

    begin = place * z.share - tap * z.chan
    if z.share % 8 == 0 and z.chan % 8 == 0:
        out[...] = rows_out[pl.ds(pl.multiple_of(begin, 8), z.share), :]
    else:
        size = -(-(z.share + 7) // 8) * 8
        rest = lax.rem(begin, 8)
        block = rows_out[pl.ds(pl.multiple_of(begin - rest, 8), size), :]
        out[...] = pltpu.roll(block, lax.rem(size - rest, size), 0)[: z.share]


def call(body, outs, spaces, scratch=()):
    kinds = dict(s=pltpu.SMEM, h=pltpu.HBM, v=pltpu.VMEM)
    single = not isinstance(outs, (list, tuple))
    vmem = pl.BlockSpec(memory_space=pltpu.VMEM)
    return pl.pallas_call(
        body,
        out_shape=outs,
        in_specs=[pl.BlockSpec(memory_space=kinds[k]) for k in spaces],
        out_specs=vmem if single else [vmem] * len(outs),
        scratch_shapes=list(scratch),
        compiler_params=pltpu.CompilerParams(vmem_limit_bytes=40 * 2**20),
    )


def on_device(images, targets, kernels):
    kernel = kernels[0]
    dp = lax.axis_size("dp")
    n_section = lax.axis_size("section")
    z = Sizes(images, kernel, dp)
    sel = {k: jnp.asarray(v, BF) for k, v in selectors(z).items()}
    scale = 1.0 / (z.micro * dp * images.shape[1])
    where = jnp.stack([lax.axis_index("section"), lax.axis_index("dp")]).astype(jnp.int32)
    image_rows = images.reshape(z.micro * z.fine, z.chan)
    target_rows = targets.reshape(z.micro, z.fine, z.chan)
    rows, width, both = z.rows, z.width, z.both

    def shape(*dims, dtype=BF):
        return jax.ShapeDtypeStruct(dims, dtype)

    join = pltpu.VMEM((2, rows, width), F32)
    buffer = pltpu.VMEM((z.taps_rows, width), BF)
    sems = pltpu.SemaphoreType.DMA((9,))

    def across(x, bit):
        return lax.ppermute(x, "section", [(s, s ^ bit) for s in range(n_section)])

    def spread(x):
        return lax.all_to_all(x, "dp", 0, 0, tiled=True)

    other = across(kernel, 1)
    encoded, patches = call(
        functools.partial(encoder_kernel, z),
        [shape(2 * z.micro, rows, width), shape(9, both, width)],
        "hvv",
        [buffer, sems],
    )(kernel, image_rows, sel["enc"])
    encoded_in = across(encoded, 1)
    forward, centre_slope, enc_slope = call(
        functools.partial(centre_kernel, z),
        [shape(2, rows, width), shape(rows, width, dtype=F32), shape(rows, width, dtype=F32)],
        "shhvvv",
        [buffer, sems],
    )(where, kernel, other, encoded, encoded_in, sel["shift"])
    forward_in = across(forward, 2)
    grads, middle_own, middle_send = call(
        functools.partial(middle_kernel, z, scale),
        [shape(2, rows, width), shape(10, rows, width), shape(9, rows, width)],
        "shhvvvvvv",
        [
            join,
            pltpu.VMEM((4 * rows, z.low), F32),
            pltpu.VMEM((4 * rows, z.low), F32),
            pltpu.VMEM((9 * rows, z.low), BF),
            pltpu.VMEM((9 * rows, z.width - z.high), BF),
            buffer,
            buffer,
            sems,
            sems,
        ],
    )(
        where, kernel, other, forward_in, target_rows,
        sel["shift"], sel["back"], sel["parity"], sel["gather"],
    )
    grads_in = across(grads, 2)
    middle_in = across(middle_send, 1)
    first, joined = call(
        functools.partial(prepare_first_kernel, z),
        [shape(dp, both, width), shape(dp, rows, width)],
        "svvvvv",
    )(where, patches, encoded, encoded_in, middle_own, middle_in)
    left = spread(first)
    back_own, back_send = call(
        functools.partial(centre_back_kernel, z),
        [shape(rows, width), shape(rows, width)],
        "shhvvvv",
        [join, buffer, sems],
    )(where, kernel, other, grads_in, enc_slope, centre_slope, sel["back"])
    back_in = across(back_send, 1)
    second = call(functools.partial(prepare_second_kernel, z), shape(dp, both, width), "svvvv")(
        where, back_own, back_in, middle_own, middle_in
    )
    right = spread(second)
    joined = spread(joined)
    joined_in = across(joined, 1)
    out = call(
        functools.partial(weight_kernel, z),
        shape(z.share, width, dtype=F32),
        "svvvvv",
        [pltpu.VMEM((dp * both, width), BF), pltpu.VMEM((2 * z.chan, width), F32)],
    )(where, sel["shift"], left, right, joined, joined_in)
    return out[None]


def solution(mesh):
    return jax.shard_map(
        on_device,
        mesh=mesh,
        in_specs=(P(None, "dp", None, None), P(None, "dp", None, None), P("section", None, None)),
        out_specs=P("section", "dp", None),
        check_vma=False,
    )
```

```python
import functools

import jax
import jax.numpy as jnp
import numpy as np
from jax import lax
from jax.experimental import pallas as pl
from jax.experimental.pallas import tpu as pltpu
from jax.sharding import PartitionSpec as P


BF = jnp.bfloat16
F32 = jnp.float32
TAPS = [(a, b) for a in range(3) for b in range(3)]
PARITIES = [(r, s) for r in range(2) for s in range(2)]


def offset_of(parity, tap):
    return (parity + tap - 1) // 2


def dot(left, right, dims=((1,), (0,))):
    return lax.dot_general(left, right, (dims, ((), ())), preferred_element_type=F32)


def dot_nt(left, right):
    return dot(left, right, ((1,), (1,)))


def dot_tn(left, right):
    return dot(left, right, ((0,), (0,)))


def sigmoid(v):
    return 1.0 / (1.0 + jnp.exp(-v))


def silu(v):
    return v * sigmoid(v)


def slope(v):
    g = sigmoid(v)
    return g * (1.0 + v * (1.0 - g))


class Sizes:
    def __init__(self, images, kernel, dp):
        self.micro = images.shape[0]
        self.full = images.shape[2]
        self.half = self.full // 2
        self.taps_rows, self.width = kernel.shape
        self.chan = self.taps_rows // 9
        self.cells = self.half * self.half
        self.rows = -(-self.cells // 8) * 8
        self.both = self.micro * self.rows
        self.packed = -(-self.micro * self.cells // 8) * 8
        self.group = self.width // 2
        self.low = -(-self.group // 128) * 128
        self.high = self.group // 128 * 128
        self.fine = self.full * self.full
        self.dp = dp
        self.share = self.taps_rows // dp


def selectors(z):
    rows, n = z.rows, z.half
    shift = np.zeros((9, rows, rows), np.float32)
    enc = np.zeros((9, z.micro, rows, z.micro, z.fine), np.float32)
    parity = np.zeros((4, rows, z.fine), np.float32)
    gather = np.zeros((9, rows, 4, rows), np.float32)
    for i in range(n):
        for j in range(n):
            r = i * n + j
            for t, (a, b) in enumerate(TAPS):
                ii, jj = i + a - 1, j + b - 1
                if 0 <= ii < n and 0 <= jj < n:
                    shift[t, r, ii * n + jj] = 1
                ii, jj = 2 * i + a - 1, 2 * j + b - 1
                if 0 <= ii < z.full and 0 <= jj < z.full:
                    for m in range(z.micro):
                        enc[t, m, r, m, ii * z.full + jj] = 1
                for p, (pr, ps) in enumerate(PARITIES):
                    ii, jj = i + offset_of(pr, a), j + offset_of(ps, b)
                    if 0 <= ii < n and 0 <= jj < n:
                        gather[t, ii * n + jj, p, r] = 1
            for p, (pr, ps) in enumerate(PARITIES):
                parity[p, r, (2 * i + pr) * z.full + 2 * j + ps] = 1
    back = shift.transpose(0, 2, 1)
    many = np.zeros((9, z.packed, z.packed), np.float32)
    for m in range(z.micro):
        at = slice(m * z.cells, (m + 1) * z.cells)
        many[:, at, at] = shift[:, : z.cells, : z.cells]
    return dict(
        many=many.reshape(9 * z.packed, z.packed),
        shift=shift.reshape(9 * rows, rows),
        back=back.reshape(9 * rows, rows),
        enc=enc.reshape(9 * z.both, z.micro * z.fine),
        parity=parity.reshape(4 * rows, z.fine),
        gather=gather.reshape(9 * rows, 4 * rows),
    )


def lanes(shape):
    return lax.broadcasted_iota(jnp.int32, shape, 1)


def join_columns(z, first, second):
    overlap = z.low - z.high
    if overlap == 0:
        return jnp.concatenate([first, second], axis=1)
    mid_first = first[:, z.high :]
    mid = jnp.where(lanes(mid_first.shape) < z.group - z.high, mid_first, second[:, :overlap])
    return jnp.concatenate([first[:, : z.high], mid, second[:, overlap:]], axis=1)


def split_groups(z, value):
    swapped = pltpu.roll(value.astype(F32), z.group, 1).astype(BF)
    return value[:, : z.group], swapped[:, : z.group]


def tap_rows(z, t):
    return slice(t * z.rows, (t + 1) * z.rows)


class Weights:
    def __init__(self, z, mine, own, other, buffer, sems):
        self.z, self.buffer, self.seen = z, buffer, set()

        def copies(source):
            for t in range(9):
                rows = pl.ds(t * z.chan, z.chan)
                yield pltpu.make_async_copy(source.at[rows], buffer.at[rows], sems.at[t])

        self.waits = list(copies(own))
        if mine is None:
            for copy in self.waits:
                copy.start()
            return

        @pl.when(mine)
        def _():
            for copy in copies(own):
                copy.start()

        @pl.when(jnp.logical_not(mine))
        def _():
            for copy in copies(other):
                copy.start()

    def tap(self, t, columns=slice(None)):
        if t not in self.seen:
            self.seen.add(t)
            self.waits[t].wait()
        return self.buffer[pl.ds(t * self.z.chan, self.z.chan), columns]

    def first(self, t):
        return self.tap(t, slice(0, self.z.low))

    def second(self, t):
        return self.tap(t, slice(self.z.high, self.z.width))


def conv_forward(z, value, weights, shift):
    first, second = split_groups(z, value)
    first = dot(shift[...], first).astype(BF)
    second = dot(shift[...], second).astype(BF)
    total_first = total_second = None
    for t in range(9):
        a = dot(first[tap_rows(z, t)], weights.first(t))
        b = dot(second[tap_rows(z, t)], weights.second(t))
        total_first = a if total_first is None else total_first + a
        total_second = b if total_second is None else total_second + b
    return join_columns(z, total_first, total_second)


def join_groups(z, first, second, scratch):
    scratch[0, :, : z.group] = first
    scratch[1, :, : z.group] = second
    left = scratch[0]
    right = pltpu.roll(scratch[1], z.group, 1)
    return jnp.where(lanes(left.shape) < z.group, left, right)


def rows_times_kernel(z, first, second, weights, scratch):
    total_first = total_second = None
    for t in range(9):
        a = dot_nt(first[tap_rows(z, t)], weights.first(t))
        b = dot_nt(second[tap_rows(z, t)], weights.second(t))
        total_first = a if total_first is None else total_first + a
        total_second = b if total_second is None else total_second + b
    return join_groups(z, total_first, total_second, scratch)


def conv_backward(z, delta, weights, back, scratch):
    first = delta[:, : z.low].astype(F32)
    first = jnp.where(lanes(first.shape) < z.group, first, 0.0).astype(BF)
    second = delta[:, z.high :].astype(F32)
    second = jnp.where(lanes(second.shape) >= z.group - z.high, second, 0.0).astype(BF)
    first = dot(back[...], first).astype(BF)
    second = dot(back[...], second).astype(BF)
    return rows_times_kernel(z, first, second, weights, scratch)


def encoder_kernel(z, kernel, enc, images, out, patches_out, buffer, moves, sems, move_sem):
    fetch = pltpu.make_async_copy(enc, moves, move_sem)
    fetch.start()
    weights = Weights(z, None, kernel, None, buffer, sems)
    fetch.wait()
    columns = dot(moves[...], images[...]).astype(BF)
    total = None
    for t in range(9):
        part = columns[t * z.both : (t + 1) * z.both]
        patches_out[t, :, : z.chan] = part
        a = dot(part, weights.tap(t))
        total = a if total is None else total + a
    encoded = silu(total).astype(BF)
    steep = slope(total).astype(BF)
    for m in range(z.micro):
        out[m] = encoded[m * z.rows : (m + 1) * z.rows]
        out[z.micro + m] = steep[m * z.rows : (m + 1) * z.rows]


def centre_kernel(z, where, kernel, other, own, received, shift, out, slope_out, enc_slope_out, buffer, sems):
    odd = lax.rem(where[0], 2) == 1
    weights = Weights(z, odd, kernel, other, buffer, sems)
    value = jnp.where(odd, received[1].astype(F32), own[0].astype(F32)).astype(BF)
    enc_slope_out[...] = jnp.where(odd, received[3].astype(F32), own[2].astype(F32))
    preact = conv_forward(z, value, weights, shift)
    out[0] = value
    out[1] = (value.astype(F32) + silu(preact)).astype(BF)
    slope_out[...] = slope(preact)


def middle_kernel(
    z, where, kernel, other, inbound, targets, shift, back, parity, gather,
    grads, own_out, send, scratch, delta_p, delta_q, sums_p, sums_q, buffer2, buffer3, sems2, sems3, *, scale,
):
    odd = lax.rem(where[0], 2) == 1
    centre = Weights(z, jnp.logical_not(odd), kernel, other, buffer2, sems2)
    decoder = Weights(z, odd, kernel, other, buffer3, sems3)
    scratch[...] = jnp.zeros_like(scratch)
    encoded = inbound[0]
    hidden = inbound[1]
    preact = conv_forward(z, hidden, centre, shift)
    hidden3 = (hidden.astype(F32) + silu(preact)).astype(BF)
    joined = (hidden3.astype(F32) + encoded.astype(F32)).astype(BF)
    first, second = split_groups(z, joined)
    first = dot(shift[...], first).astype(BF)
    second = dot(shift[...], second).astype(BF)
    total_p = [None] * 4
    total_q = [None] * 4
    for t, (a, b) in enumerate(TAPS):
        shifts = sorted({(offset_of(r, a), offset_of(s, b)) for r, s in PARITIES})
        blocks = [tap_rows(z, (i + 1) * 3 + j + 1) for i, j in shifts]
        left_p = jnp.concatenate([first[block] for block in blocks], axis=0)
        left_q = jnp.concatenate([second[block] for block in blocks], axis=0)
        part_p = dot(left_p, decoder.first(t))
        part_q = dot(left_q, decoder.second(t))
        for p, (r, s) in enumerate(PARITIES):
            at = tap_rows(z, shifts.index((offset_of(r, a), offset_of(s, b))))
            total_p[p] = part_p[at] if total_p[p] is None else total_p[p] + part_p[at]
            total_q[p] = part_q[at] if total_q[p] is None else total_q[p] + part_q[at]
    wanted = dot(parity[...], targets[lax.rem(where[0], 2)])
    move = z.group - z.high
    delta_p[...] = jnp.zeros_like(delta_p)
    delta_q[...] = jnp.zeros_like(delta_q)
    for p in range(4):
        value = total_p[p][:, : z.group]
        gate = total_q[p]
        if move:
            gate = pltpu.roll(gate, z.low - move, 1)
        gate = gate[:, : z.group]
        act = silu(gate)
        residual = (value * act - wanted[tap_rows(z, p)]) * scale
        delta_p[tap_rows(z, p), : z.group] = residual * act
        delta_q[tap_rows(z, p), : z.group] = residual * value * slope(gate)
    moved = delta_q[...]
    if move:
        moved = pltpu.roll(moved, move, 1)
    sums_p[...] = dot(gather[...], delta_p[...].astype(BF)).astype(BF)
    sums_q[...] = dot(gather[...], moved.astype(BF)).astype(BF)
    grad = rows_times_kernel(z, sums_p, sums_q, decoder, scratch).astype(BF)
    delta = (grad.astype(F32) * slope(preact)).astype(BF)
    flow = conv_backward(z, delta, centre, back, scratch)
    grads[0] = (grad.astype(F32) + flow).astype(BF)
    grads[1] = grad

    def sums(t):
        part_p = sums_p[tap_rows(z, t)].astype(F32)
        part_q = sums_q[tap_rows(z, t)].astype(F32)
        return join_columns(z, part_p, part_q).astype(BF)

    for t in range(9):
        here = sums(t)
        own_out[t] = here
        send[t] = here
    own_out[9] = joined
    send[9] = joined
    own_out[10] = delta
    send[10] = delta


def centre_back_kernel(
    z, where, kernel, other, grads, enc_slope, centre_slope, back, own_out, send, scratch, buffer, sems
):
    odd = lax.rem(where[0], 2) == 1
    weights = Weights(z, odd, kernel, other, buffer, sems)
    scratch[...] = jnp.zeros_like(scratch)
    above = grads[0].astype(F32)
    delta = (above * centre_slope[...]).astype(BF)
    flow = conv_backward(z, delta, weights, back, scratch)
    below = (above + flow).astype(BF)
    total = below.astype(F32) + grads[1].astype(F32)
    deep = total * enc_slope[...]
    own_out[...] = jnp.where(odd, delta.astype(F32), deep).astype(BF)
    send[...] = jnp.where(odd, deep, delta.astype(F32)).astype(BF)


def first_tap(z, dest):
    return dest * z.share // z.chan


def pack(z, scratch, top, bottom):
    scratch[: z.rows] = top.astype(F32)
    scratch[z.cells : z.cells + z.rows] = bottom.astype(F32)
    return scratch[: z.packed].astype(BF)


def prepare_zero_kernel(z, where, patches, inbound, out):
    section = where[0]
    n, rows = z.dp, z.rows
    mine = pl.ds(pl.multiple_of(lax.rem(section, 2) * rows, 8), rows)

    @pl.when(section < 2)
    def _():
        for k in range(n):
            tap = first_tap(z, k)
            near = patches[tap, mine].astype(F32)
            far = patches[min(tap + 1, 8), mine].astype(F32)
            both = jnp.where(lanes(near.shape) < z.chan, near, pltpu.roll(far, z.chan, 1))
            out[k] = both.astype(BF)

    @pl.when(section >= 2)
    def _():
        for k in range(n):
            out[k] = inbound[1]


def prepare_first_kernel(z, where, encoded, own, received, out, scratch):
    section = where[0]
    n = z.dp

    def fill(top, bottom):
        both = pack(z, scratch, top, bottom)
        for k in range(n):
            out[k] = both

    pl.when(section < 2)(lambda: fill(encoded[0], encoded[1]))
    pl.when(section == 3)(lambda: fill(received[9], own[9]))

    @pl.when(section == 2)
    def _():
        for k in range(n):
            tap = first_tap(z, k)
            out[k] = pack(z, scratch, own[tap], received[tap])


def prepare_second_kernel(z, where, back_own, back_received, middle_own, middle_received, out, scratch):
    section = where[0]
    n = z.dp

    def fill(top, bottom):
        both = pack(z, scratch, top[...], bottom[...])
        for k in range(n):
            out[k] = both

    pl.when(section == 0)(lambda: fill(back_own, back_received))
    pl.when(section == 1)(lambda: fill(back_received, back_own))
    pl.when(section == 2)(lambda: fill(middle_own.at[10], middle_received.at[10]))

    @pl.when(section == 3)
    def _():
        for k in range(n):
            tap = min(first_tap(z, k) + 1, 8)
            out[k] = pack(z, scratch, middle_received[tap], middle_own[tap])


def grouped(z, a, b):
    first = dot_tn(a[:, : z.low], b[:, : z.low])
    second = dot_tn(a[:, z.high :], b[:, z.high :])
    move = z.group - z.high
    return join_columns(z, first[: z.chan], second[move : move + z.chan])


def left_kernel(z, where, many, zero, zero_other, one, one_other, lefts, early, scratch):
    n = z.dp
    section, place = where[0], where[1]
    tap = first_tap(z, place)

    def rows_of(k):
        return pl.ds(k * z.packed, z.packed)

    def moved(value_of):
        for k in range(n):
            value = value_of(k)
            for at in range(2):
                here = jnp.minimum(tap + at, 8)
                move = many[pl.ds(pl.multiple_of(here * z.packed, 8), z.packed), :]
                lefts[at, rows_of(k), :] = dot(move, value).astype(BF)

    @pl.when(section == 0)
    def _():
        for k in range(n):
            lefts[0, rows_of(k), :] = pack(z, scratch, zero[k], zero_other[k])

    pl.when(section == 1)(lambda: moved(lambda k: one[k]))
    pl.when(section == 2)(lambda: moved(lambda k: pack(z, scratch, zero[k], zero_other[k])))

    @pl.when(section == 3)
    def _():
        for k in range(n):
            lefts[0, rows_of(k), :] = one[k]
        early[...] = grouped(z, lefts[0], one_other[...].reshape(n * z.packed, z.width))


def weight_kernel(z, where, right, lefts, early, out, rows_out):
    n = z.dp
    section, place = where[0], where[1]
    tap = first_tap(z, place)
    b = right[...].reshape(n * z.packed, z.width)

    @pl.when(section == 0)
    def _():
        rows_out[...] = dot_tn(lefts[0], b)

    @pl.when(jnp.logical_or(section == 1, section == 2))
    def _():
        for at in range(2):
            rows_out[pl.ds(at * z.chan, z.chan), :] = grouped(z, lefts[at], b)

    @pl.when(section == 3)
    def _():
        rows_out[: z.chan] = early[...]
        rows_out[z.chan :] = grouped(z, lefts[0], b)

    begin = place * z.share - tap * z.chan
    if z.share % 8 == 0 and z.chan % 8 == 0:
        out[...] = rows_out[pl.ds(pl.multiple_of(begin, 8), z.share), :]
    else:
        size = -(-(z.share + 7) // 8) * 8
        rest = lax.rem(begin, 8)
        block = rows_out[pl.ds(pl.multiple_of(begin - rest, 8), size), :]
        out[...] = pltpu.roll(block, lax.rem(size - rest, size), 0)[: z.share]


def call(body, outs, spaces, scratch=(), flops=10**8, limit=None):
    kinds = dict(s=pltpu.SMEM, h=pltpu.HBM, v=pltpu.VMEM)
    single = not isinstance(outs, (list, tuple))
    vmem = pl.BlockSpec(memory_space=pltpu.VMEM)
    return pl.pallas_call(
        body,
        out_shape=outs,
        in_specs=[pl.BlockSpec(memory_space=kinds[k]) for k in spaces],
        out_specs=vmem if single else [vmem] * len(outs),
        scratch_shapes=list(scratch),
        cost_estimate=pl.CostEstimate(flops=flops, bytes_accessed=4 * 2**20, transcendentals=0),
        compiler_params=pltpu.CompilerParams(vmem_limit_bytes=limit),
    )


def on_device(images, targets, kernels):
    kernel = kernels[0]
    dp = lax.axis_size("dp")
    n_section = lax.axis_size("section")
    z = Sizes(images, kernel, dp)
    sel = {k: jnp.asarray(v, BF) for k, v in selectors(z).items()}
    scale = 1.0 / (z.micro * dp * images.shape[1])
    where = jnp.stack([lax.axis_index("section"), lax.axis_index("dp")]).astype(jnp.int32)
    image_rows = images.reshape(z.micro * z.fine, z.chan)
    target_rows = targets.reshape(z.micro, z.fine, z.chan)
    rows, width, both = z.rows, z.width, z.both

    def shape(*dims, dtype=BF):
        return jax.ShapeDtypeStruct(dims, dtype)

    join = pltpu.VMEM((2, rows, width), F32)
    packing = pltpu.VMEM((both, width), F32)
    buffer = pltpu.VMEM((z.taps_rows, width), BF)
    sems = pltpu.SemaphoreType.DMA((9,))
    message = shape(dp, z.packed, width)
    small = 16 * 2**20

    def across(x, bit):
        return lax.ppermute(x, "section", [(s, s ^ bit) for s in range(n_section)])

    def spread(x):
        return lax.all_to_all(x, "dp", 0, 0, tiled=True)

    def run(body, outs, spaces, scratch, *operands, **options):
        return call(functools.partial(body, z), outs, spaces, scratch, **options)(*operands)

    other = across(kernel, 1)
    encoded, patches = run(
        encoder_kernel,
        [shape(2 * z.micro, rows, width), shape(9, both, width)],
        "hhv",
        [buffer, pltpu.VMEM((9 * both, z.micro * z.fine), BF), sems, pltpu.SemaphoreType.DMA],
        kernel, sel["enc"], image_rows,
    )
    encoded_in = across(encoded, 1)
    forward, centre_slope, enc_slope = run(
        centre_kernel,
        [shape(2, rows, width), shape(rows, width, dtype=F32), shape(rows, width, dtype=F32)],
        "shhvvv",
        [buffer, sems],
        where, kernel, other, encoded, encoded_in, sel["shift"],
    )
    forward_in = across(forward, 2)
    zero = run(
        prepare_zero_kernel, shape(dp, rows, width), "svv", [],
        where, patches, forward_in, limit=small,
    )
    zero = spread(zero)
    grads, middle_own, middle_send = run(
        functools.partial(middle_kernel, scale=scale),
        [shape(2, rows, width), shape(11, rows, width), shape(11, rows, width)],
        "shhvvvvvv",
        [
            join,
            pltpu.VMEM((4 * rows, z.low), F32),
            pltpu.VMEM((4 * rows, z.low), F32),
            pltpu.VMEM((9 * rows, z.low), BF),
            pltpu.VMEM((9 * rows, z.width - z.high), BF),
            buffer,
            buffer,
            sems,
            sems,
        ],
        where, kernel, other, forward_in, target_rows,
        sel["shift"], sel["back"], sel["parity"], sel["gather"],
        flops=10**10,
    )
    grads_in = across(grads, 2)
    middle_in = across(middle_send, 1)
    one = run(
        prepare_first_kernel, message, "svvv", [packing],
        where, encoded_in, middle_own, middle_in, limit=small,
    )
    one = spread(one)
    back_own, back_send = run(
        centre_back_kernel,
        [shape(rows, width), shape(rows, width)],
        "shhvvvv",
        [join, buffer, sems],
        where, kernel, other, grads_in, enc_slope, centre_slope, sel["back"],
        flops=10**10,
    )
    back_in = across(back_send, 1)
    right = run(
        prepare_second_kernel, message, "svvvv", [packing],
        where, back_own, back_in, middle_own, middle_in, limit=small,
    )
    right = spread(right)
    zero_other = across(zero, 1)
    one_other = across(one, 1)
    lefts, early = run(
        left_kernel,
        [shape(2, dp * z.packed, width), shape(z.chan, width, dtype=F32)],
        "svvvvv",
        [packing],
        where, sel["many"], zero, zero_other, one, one_other,
        flops=10**10, limit=2 * small,
    )
    out = run(
        weight_kernel,
        shape(z.share, width, dtype=F32),
        "svvv",
        [pltpu.VMEM((2 * z.chan, width), F32)],
        where, right, lefts, early, limit=2 * small,
    )
    return out[None]


def solution(mesh):
    return jax.shard_map(
        on_device,
        mesh=mesh,
        in_specs=(P(None, "dp", None, None), P(None, "dp", None, None), P("section", None, None)),
        out_specs=P("section", "dp", None),
        check_vma=False,
    )
```

```python
import functools

import jax
import jax.numpy as jnp
import numpy as np
from jax import lax
from jax.experimental import pallas as pl
from jax.experimental.pallas import tpu as pltpu
from jax.sharding import PartitionSpec as P


LIMIT = None
BF = jnp.bfloat16
F32 = jnp.float32
TAPS = [(a, b) for a in range(3) for b in range(3)]
PARITIES = [(r, s) for r in range(2) for s in range(2)]


def offset_of(parity, tap):
    return (parity + tap - 1) // 2


def dot(left, right, dims=((1,), (0,))):
    return lax.dot_general(left, right, (dims, ((), ())), preferred_element_type=F32)


def dot_nt(left, right):
    return dot(left, right, ((1,), (1,)))


def dot_tn(left, right):
    return dot(left, right, ((0,), (0,)))


def sigmoid(v):
    return 1.0 / (1.0 + jnp.exp(-v))


def silu(v):
    return v * sigmoid(v)


def slope(v):
    g = sigmoid(v)
    return g * (1.0 + v * (1.0 - g))


class Sizes:
    def __init__(self, images, kernel, dp):
        self.micro = images.shape[0]
        self.full = images.shape[2]
        self.half = self.full // 2
        self.taps_rows, self.width = kernel.shape
        self.chan = self.taps_rows // 9
        self.cells = self.half * self.half
        self.rows = -(-self.cells // 8) * 8
        self.both = self.micro * self.rows
        self.packed = -(-self.micro * self.cells // 8) * 8
        self.group = self.width // 2
        self.low = -(-self.group // 128) * 128
        self.high = self.group // 128 * 128
        self.fine = self.full * self.full
        self.dp = dp
        self.share = self.taps_rows // dp


def selectors(z):
    rows, n = z.rows, z.half
    shift = np.zeros((9, rows, rows), np.float32)
    parity = np.zeros((4, rows, z.fine), np.float32)
    gather = np.zeros((9, rows, 4, rows), np.float32)
    for i in range(n):
        for j in range(n):
            r = i * n + j
            for t, (a, b) in enumerate(TAPS):
                ii, jj = i + a - 1, j + b - 1
                if 0 <= ii < n and 0 <= jj < n:
                    shift[t, r, ii * n + jj] = 1
                for p, (pr, ps) in enumerate(PARITIES):
                    ii, jj = i + offset_of(pr, a), j + offset_of(ps, b)
                    if 0 <= ii < n and 0 <= jj < n:
                        gather[t, ii * n + jj, p, r] = 1
            for p, (pr, ps) in enumerate(PARITIES):
                parity[p, r, (2 * i + pr) * z.full + 2 * j + ps] = 1
    back = shift.transpose(0, 2, 1)
    many = np.zeros((9, z.packed, z.packed), np.float32)
    for m in range(z.micro):
        at = slice(m * z.cells, (m + 1) * z.cells)
        many[:, at, at] = shift[:, : z.cells, : z.cells]
    return dict(
        many=many.reshape(9 * z.packed, z.packed),
        shift=shift.reshape(9 * rows, rows),
        back=back.reshape(9 * rows, rows),
        parity=parity.reshape(4 * rows, z.fine),
        gather=gather.reshape(9 * rows, 4 * rows),
    )


def sources_of(z):
    table = np.full((z.both, 9), -1, np.int32)
    for m in range(z.micro):
        for i in range(z.half):
            for j in range(z.half):
                for t, (a, b) in enumerate(TAPS):
                    ii, jj = 2 * i + a - 1, 2 * j + b - 1
                    if ii >= 0 and jj >= 0:
                        table[m * z.rows + i * z.half + j, t] = (m * z.full + ii) * z.full + jj
    return table


def lanes(shape):
    return lax.broadcasted_iota(jnp.int32, shape, 1)


def join_columns(z, first, second):
    overlap = z.low - z.high
    if overlap == 0:
        return jnp.concatenate([first, second], axis=1)
    mid_first = first[:, z.high :]
    mid = jnp.where(lanes(mid_first.shape) < z.group - z.high, mid_first, second[:, :overlap])
    return jnp.concatenate([first[:, : z.high], mid, second[:, overlap:]], axis=1)


def split_groups(z, value):
    swapped = pltpu.roll(value.astype(F32), z.group, 1).astype(BF)
    return value[:, : z.group], swapped[:, : z.group]


def tap_rows(z, t):
    return slice(t * z.rows, (t + 1) * z.rows)


class Weights:
    def __init__(self, z, mine, own, other, buffer, sems, ahead=2):
        self.z, self.mine, self.own, self.other = z, mine, own, other
        self.buffer, self.sems, self.ahead, self.started, self.seen = buffer, sems, ahead, 0, set()
        for _ in range(ahead):
            self.start()

    def copy(self, source, t):
        rows = pl.ds(t * self.z.chan, self.z.chan)
        return pltpu.make_async_copy(source.at[rows], self.buffer.at[rows], self.sems.at[t])

    def start(self):
        t = self.started
        if t == 9:
            return
        self.started = t + 1
        if self.mine is None:
            self.copy(self.own, t).start()
            return
        pl.when(self.mine)(lambda: self.copy(self.own, t).start())
        pl.when(jnp.logical_not(self.mine))(lambda: self.copy(self.other, t).start())

    def tap(self, t, columns=slice(None)):
        if t not in self.seen:
            self.seen.add(t)
            self.copy(self.own, t).wait()
            self.start()
        return self.buffer[pl.ds(t * self.z.chan, self.z.chan), columns]

    def first(self, t):
        return self.tap(t, slice(0, self.z.low))

    def second(self, t):
        return self.tap(t, slice(self.z.high, self.z.width))


def conv_forward(z, value, weights, shift):
    first, second = split_groups(z, value)
    first = dot(shift[...], first).astype(BF)
    second = dot(shift[...], second).astype(BF)
    total_first = total_second = None
    for t in range(9):
        a = dot(first[tap_rows(z, t)], weights.first(t))
        b = dot(second[tap_rows(z, t)], weights.second(t))
        total_first = a if total_first is None else total_first + a
        total_second = b if total_second is None else total_second + b
    return join_columns(z, total_first, total_second)


def join_groups(z, first, second, scratch):
    scratch[0, :, : z.group] = first
    scratch[1, :, : z.group] = second
    left = scratch[0]
    right = pltpu.roll(scratch[1], z.group, 1)
    return jnp.where(lanes(left.shape) < z.group, left, right)


def rows_times_kernel(z, first, second, weights, scratch):
    total_first = total_second = None
    for t in range(9):
        a = dot_nt(first[tap_rows(z, t)], weights.first(t))
        b = dot_nt(second[tap_rows(z, t)], weights.second(t))
        total_first = a if total_first is None else total_first + a
        total_second = b if total_second is None else total_second + b
    return join_groups(z, total_first, total_second, scratch)


def conv_backward(z, delta, weights, back, scratch):
    first = delta[:, : z.low].astype(F32)
    first = jnp.where(lanes(first.shape) < z.group, first, 0.0).astype(BF)
    second = delta[:, z.high :].astype(F32)
    second = jnp.where(lanes(second.shape) >= z.group - z.high, second, 0.0).astype(BF)
    first = dot(back[...], first).astype(BF)
    second = dot(back[...], second).astype(BF)
    return rows_times_kernel(z, first, second, weights, scratch)


def encoder_kernel(z, kernel, sources, images, out, patches_out, buffer, sems):
    weights = Weights(z, None, kernel, None, buffer, sems)
    total = None
    for t in range(9):
        at = sources[:, t : t + 1]
        move = jnp.where(lanes((z.both, z.micro * z.fine)) == at, 1.0, 0.0).astype(BF)
        part = dot(move, images[...]).astype(BF)
        patches_out[t, :, : z.chan] = part
        a = dot(part, weights.tap(t))
        total = a if total is None else total + a
    encoded = silu(total).astype(BF)
    steep = slope(total).astype(BF)
    for m in range(z.micro):
        out[m] = encoded[m * z.rows : (m + 1) * z.rows]
        out[z.micro + m] = steep[m * z.rows : (m + 1) * z.rows]


def centre_kernel(
    z, where, kernel, other, own, received, shift, out, slope_out, enc_slope_out, copies_out, buffer, sems
):
    odd = lax.rem(where[0], 2) == 1
    weights = Weights(z, odd, kernel, other, buffer, sems)
    value = jnp.where(odd, received[1].astype(F32), own[0].astype(F32)).astype(BF)
    enc_slope_out[...] = jnp.where(odd, received[3].astype(F32), own[2].astype(F32))
    preact = conv_forward(z, value, weights, shift)
    hidden = (value.astype(F32) + silu(preact)).astype(BF)
    out[0] = value
    out[1] = hidden
    for k in range(z.dp):
        copies_out[k] = hidden
    slope_out[...] = slope(preact)


def middle_kernel(
    z, where, kernel, other, inbound, targets, shift, back, parity, gather, patches, mine_forward,
    grads, own_out, send, message, scratch, delta_p, delta_q, sums_p, sums_q, packing,
    buffer2, buffer3, sems2, sems3, *, scale,
):
    section = where[0]
    odd = lax.rem(section, 2) == 1
    centre = Weights(z, jnp.logical_not(odd), kernel, other, buffer2, sems2)
    decoder = Weights(z, odd, kernel, other, buffer3, sems3)
    scratch[...] = jnp.zeros_like(scratch)
    encoded = inbound[0]
    hidden = inbound[1]
    preact = conv_forward(z, hidden, centre, shift)
    hidden3 = (hidden.astype(F32) + silu(preact)).astype(BF)
    joined = (hidden3.astype(F32) + encoded.astype(F32)).astype(BF)
    first, second = split_groups(z, joined)
    first = dot(shift[...], first).astype(BF)
    second = dot(shift[...], second).astype(BF)
    total_p = [None] * 4
    total_q = [None] * 4
    for t, (a, b) in enumerate(TAPS):
        shifts = sorted({(offset_of(r, a), offset_of(s, b)) for r, s in PARITIES})
        blocks = [tap_rows(z, (i + 1) * 3 + j + 1) for i, j in shifts]
        left_p = jnp.concatenate([first[block] for block in blocks], axis=0)
        left_q = jnp.concatenate([second[block] for block in blocks], axis=0)
        part_p = dot(left_p, decoder.first(t))
        part_q = dot(left_q, decoder.second(t))
        for p, (r, s) in enumerate(PARITIES):
            at = tap_rows(z, shifts.index((offset_of(r, a), offset_of(s, b))))
            total_p[p] = part_p[at] if total_p[p] is None else total_p[p] + part_p[at]
            total_q[p] = part_q[at] if total_q[p] is None else total_q[p] + part_q[at]
    wanted = dot(parity[...], targets[lax.rem(where[0], 2)])
    move = z.group - z.high
    delta_p[...] = jnp.zeros_like(delta_p)
    delta_q[...] = jnp.zeros_like(delta_q)
    for p in range(4):
        value = total_p[p][:, : z.group]
        gate = total_q[p]
        if move:
            gate = pltpu.roll(gate, z.low - move, 1)
        gate = gate[:, : z.group]
        act = silu(gate)
        residual = (value * act - wanted[tap_rows(z, p)]) * scale
        delta_p[tap_rows(z, p), : z.group] = residual * act
        delta_q[tap_rows(z, p), : z.group] = residual * value * slope(gate)
    moved = delta_q[...]
    if move:
        moved = pltpu.roll(moved, move, 1)
    sums_p[...] = dot(gather[...], delta_p[...].astype(BF)).astype(BF)
    sums_q[...] = dot(gather[...], moved.astype(BF)).astype(BF)
    grad = rows_times_kernel(z, sums_p, sums_q, decoder, scratch).astype(BF)
    delta = (grad.astype(F32) * slope(preact)).astype(BF)
    flow = conv_backward(z, delta, centre, back, scratch)
    grads[0] = (grad.astype(F32) + flow).astype(BF)
    grads[1] = grad

    def sums(t):
        part_p = sums_p[tap_rows(z, t)].astype(F32)
        part_q = sums_q[tap_rows(z, t)].astype(F32)
        return join_columns(z, part_p, part_q).astype(BF)

    for t in range(9):
        here = sums(t)
        own_out[t] = here
        send[t] = here
    own_out[9] = delta
    send[9] = delta

    packing[...] = jnp.zeros_like(packing)

    @pl.when(section >= 2)
    def _():
        for k in range(z.dp):
            message[k] = pack(z, packing, own_out[first_tap(z, k)], joined)

    @pl.when(section < 2)
    def _():
        mine = pl.ds(pl.multiple_of(lax.rem(section, 2) * z.rows, 8), z.rows)
        for k in range(z.dp):
            tap = first_tap(z, k)
            near = patches[tap, mine].astype(F32)
            far = patches[min(tap + 1, 8), mine].astype(F32)
            both = jnp.where(lanes(near.shape) < z.chan, near, pltpu.roll(far, z.chan, 1))
            message[k] = pack(z, packing, both, mine_forward[0])


def centre_back_kernel(
    z, where, kernel, other, grads, enc_slope, centre_slope, back, own_out, send, scratch, buffer, sems
):
    odd = lax.rem(where[0], 2) == 1
    weights = Weights(z, odd, kernel, other, buffer, sems)
    scratch[...] = jnp.zeros_like(scratch)
    above = grads[0].astype(F32)
    delta = (above * centre_slope[...]).astype(BF)
    flow = conv_backward(z, delta, weights, back, scratch)
    below = (above + flow).astype(BF)
    total = below.astype(F32) + grads[1].astype(F32)
    deep = total * enc_slope[...]
    own_out[...] = jnp.where(odd, delta.astype(F32), deep).astype(BF)
    send[...] = jnp.where(odd, deep, delta.astype(F32)).astype(BF)


def first_tap(z, dest):
    return dest * z.share // z.chan


def pack(z, scratch, top, bottom):
    scratch[: z.rows] = top.astype(F32)
    scratch[z.cells : z.cells + z.rows] = bottom.astype(F32)
    return scratch[: z.packed].astype(BF)


def prepare_second_kernel(z, where, back_own, back_received, middle_own, middle_received, out, scratch):
    section = where[0]
    n = z.dp

    def fill(top, bottom):
        both = pack(z, scratch, top[...], bottom[...])
        for k in range(n):
            out[k] = both

    pl.when(section == 0)(lambda: fill(back_own, back_received))
    pl.when(section == 1)(lambda: fill(back_received, back_own))
    pl.when(section == 2)(lambda: fill(middle_own.at[9], middle_received.at[9]))

    @pl.when(section == 3)
    def _():
        for k in range(n):
            tap = min(first_tap(z, k) + 1, 8)
            out[k] = pack(z, scratch, middle_received[tap], middle_own[tap])


def grouped(z, a, b):
    first = dot_tn(a[:, : z.low], b[:, : z.low])
    second = dot_tn(a[:, z.high :], b[:, z.high :])
    move = z.group - z.high
    return join_columns(z, first[: z.chan], second[move : move + z.chan])


def left_kernel(z, where, many, zero, zero_other, one, one_other, lefts, early, scratch, first, second):
    n = z.dp
    section, place = where[0], where[1]
    tap = first_tap(z, place)

    def rows_of(k):
        return pl.ds(k * z.packed, z.packed)

    def halves(k):
        first[: z.packed] = one_other[k].astype(F32)
        second[: z.packed] = one[k].astype(F32)

    def upper(k, even_first):
        halves(k)
        top, bottom = (first, second) if even_first else (second, first)
        return pack(z, scratch, top[: z.rows], bottom[: z.rows])

    def lower(k):
        halves(k)
        here = slice(z.cells, z.cells + z.rows)
        return pack(z, scratch, first[here], second[here])

    def moved(value_of):
        for k in range(n):
            value = value_of(k)
            for at in range(2):
                here = jnp.minimum(tap + at, 8)
                move = many[pl.ds(pl.multiple_of(here * z.packed, 8), z.packed), :]
                lefts[at, rows_of(k), :] = dot(move, value).astype(BF)

    first[...] = jnp.zeros_like(first)
    second[...] = jnp.zeros_like(second)

    @pl.when(section == 0)
    def _():
        for k in range(n):
            lefts[0, rows_of(k), :] = upper(k, False)

    pl.when(section == 1)(lambda: moved(lower))
    pl.when(section == 2)(lambda: moved(lambda k: pack(z, scratch, zero[k], zero_other[k])))

    @pl.when(section == 3)
    def _():
        for k in range(n):
            lefts[0, rows_of(k), :] = lower(k)
            lefts[1, rows_of(k), :] = upper(k, True)
        early[...] = grouped(z, lefts[0], lefts[1])


def weight_kernel(z, where, right, lefts, early, out, rows_out):
    n = z.dp
    section, place = where[0], where[1]
    tap = first_tap(z, place)
    b = right[...].reshape(n * z.packed, z.width)

    @pl.when(section == 0)
    def _():
        rows_out[...] = dot_tn(lefts[0], b)

    @pl.when(jnp.logical_or(section == 1, section == 2))
    def _():
        for at in range(2):
            rows_out[pl.ds(at * z.chan, z.chan), :] = grouped(z, lefts[at], b)

    @pl.when(section == 3)
    def _():
        rows_out[: z.chan] = early[...]
        rows_out[z.chan :] = grouped(z, lefts[0], b)

    begin = place * z.share - tap * z.chan
    if z.share % 8 == 0 and z.chan % 8 == 0:
        out[...] = rows_out[pl.ds(pl.multiple_of(begin, 8), z.share), :]
    else:
        size = -(-(z.share + 7) // 8) * 8
        rest = lax.rem(begin, 8)
        block = rows_out[pl.ds(pl.multiple_of(begin - rest, 8), size), :]
        out[...] = pltpu.roll(block, lax.rem(size - rest, size), 0)[: z.share]


def call(body, outs, spaces, scratch=(), flops=10**8, limit=None):
    kinds = dict(s=pltpu.SMEM, h=pltpu.HBM, v=pltpu.VMEM)
    single = not isinstance(outs, (list, tuple))
    vmem = pl.BlockSpec(memory_space=pltpu.VMEM)
    return pl.pallas_call(
        body,
        out_shape=outs,
        in_specs=[pl.BlockSpec(memory_space=kinds[k]) for k in spaces],
        out_specs=vmem if single else [vmem] * len(outs),
        scratch_shapes=list(scratch),
        cost_estimate=pl.CostEstimate(flops=flops, bytes_accessed=4 * 2**20, transcendentals=0),
        compiler_params=pltpu.CompilerParams(vmem_limit_bytes=limit),
    )


def on_device(images, targets, kernels):
    kernel = kernels[0]
    dp = lax.axis_size("dp")
    n_section = lax.axis_size("section")
    z = Sizes(images, kernel, dp)
    sel = {k: jnp.asarray(v, BF) for k, v in selectors(z).items()}
    scale = 1.0 / (z.micro * dp * images.shape[1])
    where = jnp.stack([lax.axis_index("section"), lax.axis_index("dp")]).astype(jnp.int32)
    image_rows = images.reshape(z.micro * z.fine, z.chan)
    target_rows = targets.reshape(z.micro, z.fine, z.chan)
    rows, width, both = z.rows, z.width, z.both

    def shape(*dims, dtype=BF):
        return jax.ShapeDtypeStruct(dims, dtype)

    join = pltpu.VMEM((2, rows, width), F32)
    packing = pltpu.VMEM((both, width), F32)
    message = shape(dp, z.packed, width)
    small = 16 * 2**20
    large = LIMIT
    buffer = pltpu.VMEM((z.taps_rows, width), BF)
    sems = pltpu.SemaphoreType.DMA((9,))

    def across(x, bit):
        return lax.ppermute(x, "section", [(s, s ^ bit) for s in range(n_section)])

    def spread(x):
        return lax.all_to_all(x, "dp", 0, 0, tiled=True)

    def run(body, outs, spaces, scratch, *operands, **options):
        return call(functools.partial(body, z), outs, spaces, scratch, **options)(*operands)

    other = across(kernel, 1)
    encoded, patches = run(
        encoder_kernel,
        [shape(2 * z.micro, rows, width), shape(9, both, width)],
        "hvv",
        [buffer, sems],
        kernel, jnp.asarray(sources_of(z)), image_rows,
        limit=large,
    )
    encoded_in = across(encoded, 1)
    forward, centre_slope, enc_slope, copies = run(
        centre_kernel,
        [
            shape(2, rows, width),
            shape(rows, width, dtype=F32),
            shape(rows, width, dtype=F32),
            shape(dp, rows, width),
        ],
        "shhvvv",
        [buffer, sems],
        where, kernel, other, encoded, encoded_in, sel["shift"],
        limit=large,
    )
    forward_in = across(forward, 2)
    zero = spread(copies)
    grads, middle_own, middle_send, one = run(
        functools.partial(middle_kernel, scale=scale),
        [shape(2, rows, width), shape(10, rows, width), shape(10, rows, width), message],
        "shhvvvvvvvv",
        [
            join,
            pltpu.VMEM((4 * rows, z.low), F32),
            pltpu.VMEM((4 * rows, z.low), F32),
            pltpu.VMEM((9 * rows, z.low), BF),
            pltpu.VMEM((9 * rows, z.width - z.high), BF),
            packing,
            buffer,
            buffer,
            sems,
            sems,
        ],
        where, kernel, other, forward_in, target_rows,
        sel["shift"], sel["back"], sel["parity"], sel["gather"], patches, forward,
        flops=10**10, limit=large,
    )
    grads_in = across(grads, 2)
    one = spread(one)
    back_own, back_send = run(
        centre_back_kernel,
        [shape(rows, width), shape(rows, width)],
        "shhvvvv",
        [join, buffer, sems],
        where, kernel, other, grads_in, enc_slope, centre_slope, sel["back"],
        flops=10**10, limit=large,
    )
    back_in = across(back_send, 1)
    middle_in = across(middle_send, 1)
    right = run(
        prepare_second_kernel, message, "svvvv", [packing],
        where, back_own, back_in, middle_own, middle_in, limit=small,
    )
    right = spread(right)
    zero = across(zero, 2)
    zero_other = across(zero, 1)
    one_other = across(one, 1)
    lefts, early = run(
        left_kernel,
        [shape(2, dp * z.packed, width), shape(z.chan, width, dtype=F32)],
        "svvvvv",
        [packing, packing, packing],
        where, sel["many"], zero, zero_other, one, one_other,
        flops=10**10, limit=2 * small,
    )
    out = run(
        weight_kernel,
        shape(z.share, width, dtype=F32),
        "svvv",
        [pltpu.VMEM((2 * z.chan, width), F32)],
        where, right, lefts, early, limit=2 * small,
    )
    return out[None]


def solution(mesh):
    return jax.shard_map(
        on_device,
        mesh=mesh,
        in_specs=(P(None, "dp", None, None), P(None, "dp", None, None), P("section", None, None)),
        out_specs=P("section", "dp", None),
        check_vma=False,
    )
```

```python
import functools

import jax
import jax.numpy as jnp
import numpy as np
from jax import lax
from jax.experimental import pallas as pl
from jax.experimental.pallas import tpu as pltpu
from jax.sharding import PartitionSpec as P


LIMIT = None
BF = jnp.bfloat16
F32 = jnp.float32
TAPS = [(a, b) for a in range(3) for b in range(3)]
PARITIES = [(r, s) for r in range(2) for s in range(2)]


def offset_of(parity, tap):
    return (parity + tap - 1) // 2


def dot(left, right, dims=((1,), (0,))):
    return lax.dot_general(left, right, (dims, ((), ())), preferred_element_type=F32)


def dot_nt(left, right):
    return dot(left, right, ((1,), (1,)))


def dot_tn(left, right):
    return dot(left, right, ((0,), (0,)))


def sigmoid(v):
    return 1.0 / (1.0 + jnp.exp(-v))


def silu(v):
    return v * sigmoid(v)


def slope(v):
    g = sigmoid(v)
    return g * (1.0 + v * (1.0 - g))


class Sizes:
    def __init__(self, images, kernel, dp):
        self.micro = images.shape[0]
        self.full = images.shape[2]
        self.half = self.full // 2
        self.taps_rows, self.width = kernel.shape
        self.chan = self.taps_rows // 9
        self.cells = self.half * self.half
        self.rows = -(-self.cells // 8) * 8
        self.both = self.micro * self.rows
        self.packed = -(-self.micro * self.cells // 8) * 8
        self.group = self.width // 2
        self.low = -(-self.group // 128) * 128
        self.high = self.group // 128 * 128
        self.fine = self.full * self.full
        self.dp = dp
        self.share = self.taps_rows // dp


def selectors(z):
    rows, n = z.rows, z.half
    shift = np.zeros((9, rows, rows), np.float32)
    parity = np.zeros((4, rows, z.fine), np.float32)
    gather = np.zeros((9, rows, 4, rows), np.float32)
    for i in range(n):
        for j in range(n):
            r = i * n + j
            for t, (a, b) in enumerate(TAPS):
                ii, jj = i + a - 1, j + b - 1
                if 0 <= ii < n and 0 <= jj < n:
                    shift[t, r, ii * n + jj] = 1
                for p, (pr, ps) in enumerate(PARITIES):
                    ii, jj = i + offset_of(pr, a), j + offset_of(ps, b)
                    if 0 <= ii < n and 0 <= jj < n:
                        gather[t, ii * n + jj, p, r] = 1
            for p, (pr, ps) in enumerate(PARITIES):
                parity[p, r, (2 * i + pr) * z.full + 2 * j + ps] = 1
    back = shift.transpose(0, 2, 1)
    many = np.zeros((9, z.packed, z.packed), np.float32)
    for m in range(z.micro):
        at = slice(m * z.cells, (m + 1) * z.cells)
        many[:, at, at] = shift[:, : z.cells, : z.cells]
    return dict(
        many=many.reshape(9 * z.packed, z.packed),
        shift=shift.reshape(9 * rows, rows),
        back=back.reshape(9 * rows, rows),
        parity=parity.reshape(4 * rows, z.fine),
        gather=gather.reshape(9 * rows, 4 * rows),
    )


def sources_of(z):
    table = np.full((z.both, 9), -1, np.int32)
    for m in range(z.micro):
        for i in range(z.half):
            for j in range(z.half):
                for t, (a, b) in enumerate(TAPS):
                    ii, jj = 2 * i + a - 1, 2 * j + b - 1
                    if ii >= 0 and jj >= 0:
                        table[m * z.rows + i * z.half + j, t] = (m * z.full + ii) * z.full + jj
    return table


def lanes(shape):
    return lax.broadcasted_iota(jnp.int32, shape, 1)


def join_columns(z, first, second):
    overlap = z.low - z.high
    if overlap == 0:
        return jnp.concatenate([first, second], axis=1)
    mid_first = first[:, z.high :]
    mid = jnp.where(lanes(mid_first.shape) < z.group - z.high, mid_first, second[:, :overlap])
    return jnp.concatenate([first[:, : z.high], mid, second[:, overlap:]], axis=1)


def split_groups(z, value):
    swapped = pltpu.roll(value.astype(F32), z.group, 1).astype(BF)
    return value[:, : z.group], swapped[:, : z.group]


def tap_rows(z, t):
    return slice(t * z.rows, (t + 1) * z.rows)


class Weights:
    def __init__(self, z, mine, own, other, buffer, sem):
        self.z, self.buffer, self.there, self.started = z, buffer, False, False
        self.mine, self.own, self.other, self.sem = mine, own, other, sem

    def copy(self, source):
        return pltpu.make_async_copy(source, self.buffer, self.sem)

    def start(self):
        if self.mine is None:
            self.copy(self.own).start()
        else:
            pl.when(self.mine)(lambda: self.copy(self.own).start())
            pl.when(jnp.logical_not(self.mine))(lambda: self.copy(self.other).start())
        return self

    def wait(self):
        self.copy(self.own).wait()

    def tap(self, t, columns=slice(None)):
        return self.buffer[pl.ds(t * self.z.chan, self.z.chan), columns]

    def first(self, t):
        return self.tap(t, slice(0, self.z.low))

    def second(self, t):
        return self.tap(t, slice(self.z.high, self.z.width))


def conv_forward(z, value, weights, shift, ready=None):
    first, second = split_groups(z, value)
    first = dot(shift[...], first).astype(BF)
    second = dot(shift[...], second).astype(BF)
    if ready is not None:
        ready()
    total_first = total_second = None
    for t in range(9):
        a = dot(first[tap_rows(z, t)], weights.first(t))
        b = dot(second[tap_rows(z, t)], weights.second(t))
        total_first = a if total_first is None else total_first + a
        total_second = b if total_second is None else total_second + b
    return join_columns(z, total_first, total_second)


def join_groups(z, first, second, scratch):
    scratch[0, :, : z.group] = first
    scratch[1, :, : z.group] = second
    left = scratch[0]
    right = pltpu.roll(scratch[1], z.group, 1)
    return jnp.where(lanes(left.shape) < z.group, left, right)


def rows_times_kernel(z, first, second, weights, scratch):
    total_first = total_second = None
    for t in range(9):
        a = dot_nt(first[tap_rows(z, t)], weights.first(t))
        b = dot_nt(second[tap_rows(z, t)], weights.second(t))
        total_first = a if total_first is None else total_first + a
        total_second = b if total_second is None else total_second + b
    return join_groups(z, total_first, total_second, scratch)


def conv_backward(z, delta, weights, back, scratch, ready=None):
    first = delta[:, : z.low].astype(F32)
    first = jnp.where(lanes(first.shape) < z.group, first, 0.0).astype(BF)
    second = delta[:, z.high :].astype(F32)
    second = jnp.where(lanes(second.shape) >= z.group - z.high, second, 0.0).astype(BF)
    first = dot(back[...], first).astype(BF)
    second = dot(back[...], second).astype(BF)
    if ready is not None:
        ready()
    return rows_times_kernel(z, first, second, weights, scratch)


def encoder_kernel(z, kernel, sources, images, out, patches_out, buffer, sem):
    weights = Weights(z, None, kernel, None, buffer, sem).start()
    parts = []
    for t in range(9):
        at = sources[:, t : t + 1]
        move = jnp.where(lanes((z.both, z.micro * z.fine)) == at, 1.0, 0.0).astype(BF)
        part = dot(move, images[...]).astype(BF)
        patches_out[t, :, : z.chan] = part
        parts.append(part)
    weights.wait()
    total = None
    for t in range(9):
        a = dot(parts[t], weights.tap(t))
        total = a if total is None else total + a
    encoded = silu(total).astype(BF)
    steep = slope(total).astype(BF)
    for m in range(z.micro):
        out[m] = encoded[m * z.rows : (m + 1) * z.rows]
        out[z.micro + m] = steep[m * z.rows : (m + 1) * z.rows]


def centre_kernel(
    z, where, kernel, other, own, received, shift, out, slope_out, enc_slope_out, copies_out, buffer, sems
):
    odd = lax.rem(where[0], 2) == 1
    weights = Weights(z, odd, kernel, other, buffer, sems).start()
    value = jnp.where(odd, received[1].astype(F32), own[0].astype(F32)).astype(BF)
    enc_slope_out[...] = jnp.where(odd, received[3].astype(F32), own[2].astype(F32))
    preact = conv_forward(z, value, weights, shift, weights.wait)
    hidden = (value.astype(F32) + silu(preact)).astype(BF)
    out[0] = value
    out[1] = hidden
    for k in range(z.dp):
        copies_out[k] = hidden
    slope_out[...] = slope(preact)


def middle_kernel(
    z, where, kernel, other, inbound, targets, shift, back, parity, gather, patches, mine_forward,
    grads, own_out, send, message, scratch, delta_p, delta_q, sums_p, sums_q, packing,
    buffer2, buffer3, sems2, sems3, *, scale,
):
    section = where[0]
    odd = lax.rem(section, 2) == 1
    centre = Weights(z, jnp.logical_not(odd), kernel, other, buffer2, sems2).start()
    decoder = Weights(z, odd, kernel, other, buffer3, sems3)
    scratch[...] = jnp.zeros_like(scratch)
    encoded = inbound[0]
    hidden = inbound[1]

    def ready():
        centre.wait()
        decoder.start()

    preact = conv_forward(z, hidden, centre, shift, ready)
    hidden3 = (hidden.astype(F32) + silu(preact)).astype(BF)
    joined = (hidden3.astype(F32) + encoded.astype(F32)).astype(BF)
    first, second = split_groups(z, joined)
    first = dot(shift[...], first).astype(BF)
    second = dot(shift[...], second).astype(BF)
    decoder.wait()
    total_p = [None] * 4
    total_q = [None] * 4
    for t, (a, b) in enumerate(TAPS):
        shifts = sorted({(offset_of(r, a), offset_of(s, b)) for r, s in PARITIES})
        blocks = [tap_rows(z, (i + 1) * 3 + j + 1) for i, j in shifts]
        left_p = jnp.concatenate([first[block] for block in blocks], axis=0)
        left_q = jnp.concatenate([second[block] for block in blocks], axis=0)
        part_p = dot(left_p, decoder.first(t))
        part_q = dot(left_q, decoder.second(t))
        for p, (r, s) in enumerate(PARITIES):
            at = tap_rows(z, shifts.index((offset_of(r, a), offset_of(s, b))))
            total_p[p] = part_p[at] if total_p[p] is None else total_p[p] + part_p[at]
            total_q[p] = part_q[at] if total_q[p] is None else total_q[p] + part_q[at]
    wanted = dot(parity[...], targets[lax.rem(where[0], 2)])
    move = z.group - z.high
    delta_p[...] = jnp.zeros_like(delta_p)
    delta_q[...] = jnp.zeros_like(delta_q)
    for p in range(4):
        value = total_p[p][:, : z.group]
        gate = total_q[p]
        if move:
            gate = pltpu.roll(gate, z.low - move, 1)
        gate = gate[:, : z.group]
        act = silu(gate)
        residual = (value * act - wanted[tap_rows(z, p)]) * scale
        delta_p[tap_rows(z, p), : z.group] = residual * act
        delta_q[tap_rows(z, p), : z.group] = residual * value * slope(gate)
    moved = delta_q[...]
    if move:
        moved = pltpu.roll(moved, move, 1)
    sums_p[...] = dot(gather[...], delta_p[...].astype(BF)).astype(BF)
    sums_q[...] = dot(gather[...], moved.astype(BF)).astype(BF)
    grad = rows_times_kernel(z, sums_p, sums_q, decoder, scratch).astype(BF)
    delta = (grad.astype(F32) * slope(preact)).astype(BF)
    flow = conv_backward(z, delta, centre, back, scratch)
    grads[0] = (grad.astype(F32) + flow).astype(BF)
    grads[1] = grad

    def sums(t):
        part_p = sums_p[tap_rows(z, t)].astype(F32)
        part_q = sums_q[tap_rows(z, t)].astype(F32)
        return join_columns(z, part_p, part_q).astype(BF)

    for t in range(9):
        here = sums(t)
        own_out[t] = here
        send[t] = here
    own_out[9] = delta
    send[9] = delta

    packing[...] = jnp.zeros_like(packing)

    @pl.when(section >= 2)
    def _():
        for k in range(z.dp):
            message[k] = pack(z, packing, own_out[first_tap(z, k)], joined)

    @pl.when(section < 2)
    def _():
        mine = pl.ds(pl.multiple_of(lax.rem(section, 2) * z.rows, 8), z.rows)
        for k in range(z.dp):
            tap = first_tap(z, k)
            near = patches[tap, mine].astype(F32)
            far = patches[min(tap + 1, 8), mine].astype(F32)
            both = jnp.where(lanes(near.shape) < z.chan, near, pltpu.roll(far, z.chan, 1))
            message[k] = pack(z, packing, both, mine_forward[0])


def centre_back_kernel(
    z, where, kernel, other, grads, enc_slope, centre_slope, back, own_out, send, scratch, buffer, sems
):
    odd = lax.rem(where[0], 2) == 1
    weights = Weights(z, odd, kernel, other, buffer, sems).start()
    scratch[...] = jnp.zeros_like(scratch)
    above = grads[0].astype(F32)
    delta = (above * centre_slope[...]).astype(BF)
    flow = conv_backward(z, delta, weights, back, scratch, weights.wait)
    below = (above + flow).astype(BF)
    total = below.astype(F32) + grads[1].astype(F32)
    deep = total * enc_slope[...]
    own_out[...] = jnp.where(odd, delta.astype(F32), deep).astype(BF)
    send[...] = jnp.where(odd, deep, delta.astype(F32)).astype(BF)


def first_tap(z, dest):
    return dest * z.share // z.chan


def pack(z, scratch, top, bottom):
    scratch[: z.rows] = top.astype(F32)
    scratch[z.cells : z.cells + z.rows] = bottom.astype(F32)
    return scratch[: z.packed].astype(BF)


def prepare_second_kernel(z, where, back_own, back_received, middle_own, middle_received, out, scratch):
    section = where[0]
    n = z.dp

    def fill(top, bottom):
        both = pack(z, scratch, top[...], bottom[...])
        for k in range(n):
            out[k] = both

    pl.when(section == 0)(lambda: fill(back_own, back_received))
    pl.when(section == 1)(lambda: fill(back_received, back_own))
    pl.when(section == 2)(lambda: fill(middle_own.at[9], middle_received.at[9]))

    @pl.when(section == 3)
    def _():
        for k in range(n):
            tap = min(first_tap(z, k) + 1, 8)
            out[k] = pack(z, scratch, middle_received[tap], middle_own[tap])


def grouped(z, a, b):
    first = dot_tn(a[:, : z.low], b[:, : z.low])
    second = dot_tn(a[:, z.high :], b[:, z.high :])
    move = z.group - z.high
    return join_columns(z, first[: z.chan], second[move : move + z.chan])


def left_kernel(z, where, many, zero, zero_other, one, one_other, lefts, early, scratch, first, second):
    n = z.dp
    section, place = where[0], where[1]
    tap = first_tap(z, place)

    def rows_of(k):
        return pl.ds(k * z.packed, z.packed)

    def halves(k):
        first[: z.packed] = one_other[k].astype(F32)
        second[: z.packed] = one[k].astype(F32)

    def upper(k, even_first):
        halves(k)
        top, bottom = (first, second) if even_first else (second, first)
        return pack(z, scratch, top[: z.rows], bottom[: z.rows])

    def lower(k):
        halves(k)
        here = slice(z.cells, z.cells + z.rows)
        return pack(z, scratch, first[here], second[here])

    def moved(value_of):
        for k in range(n):
            value = value_of(k)
            for at in range(2):
                here = jnp.minimum(tap + at, 8)
                move = many[pl.ds(pl.multiple_of(here * z.packed, 8), z.packed), :]
                lefts[at, rows_of(k), :] = dot(move, value).astype(BF)

    first[...] = jnp.zeros_like(first)
    second[...] = jnp.zeros_like(second)

    @pl.when(section == 0)
    def _():
        for k in range(n):
            lefts[0, rows_of(k), :] = upper(k, False)

    pl.when(section == 1)(lambda: moved(lower))
    pl.when(section == 2)(lambda: moved(lambda k: pack(z, scratch, zero[k], zero_other[k])))

    @pl.when(section == 3)
    def _():
        for k in range(n):
            lefts[0, rows_of(k), :] = lower(k)
            lefts[1, rows_of(k), :] = upper(k, True)
        early[...] = grouped(z, lefts[0], lefts[1])


def weight_kernel(z, where, right, lefts, early, out, rows_out):
    n = z.dp
    section, place = where[0], where[1]
    tap = first_tap(z, place)
    b = right[...].reshape(n * z.packed, z.width)

    @pl.when(section == 0)
    def _():
        rows_out[...] = dot_tn(lefts[0], b)

    @pl.when(jnp.logical_or(section == 1, section == 2))
    def _():
        for at in range(2):
            rows_out[pl.ds(at * z.chan, z.chan), :] = grouped(z, lefts[at], b)

    @pl.when(section == 3)
    def _():
        rows_out[: z.chan] = early[...]
        rows_out[z.chan :] = grouped(z, lefts[0], b)

    begin = place * z.share - tap * z.chan
    if z.share % 8 == 0 and z.chan % 8 == 0:
        out[...] = rows_out[pl.ds(pl.multiple_of(begin, 8), z.share), :]
    else:
        size = -(-(z.share + 7) // 8) * 8
        rest = lax.rem(begin, 8)
        block = rows_out[pl.ds(pl.multiple_of(begin - rest, 8), size), :]
        out[...] = pltpu.roll(block, lax.rem(size - rest, size), 0)[: z.share]


def call(body, outs, spaces, scratch=(), flops=10**8, limit=None):
    kinds = dict(s=pltpu.SMEM, h=pltpu.HBM, v=pltpu.VMEM)
    single = not isinstance(outs, (list, tuple))
    vmem = pl.BlockSpec(memory_space=pltpu.VMEM)
    return pl.pallas_call(
        body,
        out_shape=outs,
        in_specs=[pl.BlockSpec(memory_space=kinds[k]) for k in spaces],
        out_specs=vmem if single else [vmem] * len(outs),
        scratch_shapes=list(scratch),
        cost_estimate=pl.CostEstimate(flops=flops, bytes_accessed=4 * 2**20, transcendentals=0),
        compiler_params=pltpu.CompilerParams(vmem_limit_bytes=limit),
    )


def on_device(images, targets, kernels):
    kernel = kernels[0]
    dp = lax.axis_size("dp")
    n_section = lax.axis_size("section")
    z = Sizes(images, kernel, dp)
    sel = {k: jnp.asarray(v, BF) for k, v in selectors(z).items()}
    scale = 1.0 / (z.micro * dp * images.shape[1])
    where = jnp.stack([lax.axis_index("section"), lax.axis_index("dp")]).astype(jnp.int32)
    image_rows = images.reshape(z.micro * z.fine, z.chan)
    target_rows = targets.reshape(z.micro, z.fine, z.chan)
    rows, width, both = z.rows, z.width, z.both

    def shape(*dims, dtype=BF):
        return jax.ShapeDtypeStruct(dims, dtype)

    join = pltpu.VMEM((2, rows, width), F32)
    packing = pltpu.VMEM((both, width), F32)
    message = shape(dp, z.packed, width)
    small = 16 * 2**20
    large = LIMIT
    buffer = pltpu.VMEM((z.taps_rows, width), BF)
    sems = pltpu.SemaphoreType.DMA

    def across(x, bit):
        return lax.ppermute(x, "section", [(s, s ^ bit) for s in range(n_section)])

    def spread(x):
        return lax.all_to_all(x, "dp", 0, 0, tiled=True)

    def run(body, outs, spaces, scratch, *operands, **options):
        return call(functools.partial(body, z), outs, spaces, scratch, **options)(*operands)

    other = across(kernel, 1)
    encoded, patches = run(
        encoder_kernel,
        [shape(2 * z.micro, rows, width), shape(9, both, width)],
        "hvv",
        [buffer, sems],
        kernel, jnp.asarray(sources_of(z)), image_rows,
        limit=large,
    )
    encoded_in = across(encoded, 1)
    forward, centre_slope, enc_slope, copies = run(
        centre_kernel,
        [
            shape(2, rows, width),
            shape(rows, width, dtype=F32),
            shape(rows, width, dtype=F32),
            shape(dp, rows, width),
        ],
        "shhvvv",
        [buffer, sems],
        where, kernel, other, encoded, encoded_in, sel["shift"],
        limit=large,
    )
    forward_in = across(forward, 2)
    zero = spread(copies)
    grads, middle_own, middle_send, one = run(
        functools.partial(middle_kernel, scale=scale),
        [shape(2, rows, width), shape(10, rows, width), shape(10, rows, width), message],
        "shhvvvvvvvv",
        [
            join,
            pltpu.VMEM((4 * rows, z.low), F32),
            pltpu.VMEM((4 * rows, z.low), F32),
            pltpu.VMEM((9 * rows, z.low), BF),
            pltpu.VMEM((9 * rows, z.width - z.high), BF),
            packing,
            buffer,
            buffer,
            sems,
            sems,
        ],
        where, kernel, other, forward_in, target_rows,
        sel["shift"], sel["back"], sel["parity"], sel["gather"], patches, forward,
        flops=10**10, limit=large,
    )
    grads_in = across(grads, 2)
    one = spread(one)
    back_own, back_send = run(
        centre_back_kernel,
        [shape(rows, width), shape(rows, width)],
        "shhvvvv",
        [join, buffer, sems],
        where, kernel, other, grads_in, enc_slope, centre_slope, sel["back"],
        flops=10**10, limit=large,
    )
    back_in = across(back_send, 1)
    middle_in = across(middle_send, 1)
    right = run(
        prepare_second_kernel, message, "svvvv", [packing],
        where, back_own, back_in, middle_own, middle_in, limit=small,
    )
    right = spread(right)
    zero = across(zero, 2)
    zero_other = across(zero, 1)
    one_other = across(one, 1)
    lefts, early = run(
        left_kernel,
        [shape(2, dp * z.packed, width), shape(z.chan, width, dtype=F32)],
        "svvvvv",
        [packing, packing, packing],
        where, sel["many"], zero, zero_other, one, one_other,
        flops=10**10, limit=2 * small,
    )
    out = run(
        weight_kernel,
        shape(z.share, width, dtype=F32),
        "svvv",
        [pltpu.VMEM((2 * z.chan, width), F32)],
        where, right, lefts, early, limit=2 * small,
    )
    return out[None]


def solution(mesh):
    return jax.shard_map(
        on_device,
        mesh=mesh,
        in_specs=(P(None, "dp", None, None), P(None, "dp", None, None), P("section", None, None)),
        out_specs=P("section", "dp", None),
        check_vma=False,
    )
```
